32 devices in a mesh: groups: 2 (over x), tiles: 16 (over z, y, core).
Axes of the slice: x: 2, y: 2, z: 4, core: 2. Of those that a mesh axis runs over, the one named last changes fastest.
Arguments:
- ocean_state: bfloat16 [32, 32, 128, 128], P(('groups', 'tiles')), parts along dimension 0, may hold values from -6 to 6
- cotangent: bfloat16 [32, 32, 128, 128], P(('groups', 'tiles')), parts along dimension 0, may hold values from -6 to 6
- first_kernel: bfloat16 [3, 3, 32, 128], replicated, may hold values from -0.375 to 0.375
- second_kernel: bfloat16 [3, 3, 32, 128], replicated, may hold values from -0.375 to 0.375
- neighbours: int32 [16, 8], P('tiles'), may hold values from -1 to 15, as said below
Outputs:
- state_grad: bfloat16 [32, 32, 128, 128], P(('groups', 'tiles')), parts along dimension 0
- first_grad: float32 [6, 3, 32, 128], P('groups'), parts along dimension 0
- second_grad: float32 [6, 3, 32, 128], P('groups'), parts along dimension 0
The draws below stay inside these ranges and needn't reach their ends.
There are 2 independent parts, one for each index of `groups`. The reference program is written for one: setup_inputs(seed, part) draws one part's arguments, and reference() takes and returns one part's arrays. A program takes and returns all parts, laid end to end along the dimension named above; an argument that names none is the same for every part. Nothing has to cross between parts.
Inputs may be any that keep to these rules, and one draw needn't show every extreme that they name: `neighbours`: ocean tiles are numbered along a curve over a grid of 4 x 5 tiles that leaves out 4 land tiles. Row t lists the tiles above, below, left, right, above left, above right, below left and below right of tile t, -1 for land or the grid's edge; the relation is symmetric; the tile above and the tile below are each t - 1 or t + 1; tiles to the right (entries 3, 5, 7) have higher numbers than t and tiles to the left (entries 2, 4, 6) lower ones; every listed tile differs from t by at most 7, and that distance is reached in every draw.
All inputs are finite; a program needn't handle non-finite values.
Results may differ from the reference program's by a relative error of at most 0.0034.
Values may be sent and summed in bfloat16 or wider, within the bound.
No kernel may reach another device: no remote copies, remote signals or barrier semaphores. Data moves between devices by JAX's collectives and lax.ppermute only.
A program may use at most 128 MiB of HBM per device.

```python
import math
import jax
import jax.numpy as jnp
from jax import lax

TH = 32
TW = 128
C = 32
GRID_ROWS = 4
LC = 128
TILES = 16
GRID_COLS = 5
LAND = 4


def draw_neighbours(key, part):
    rows_n = GRID_ROWS
    cols_n = GRID_COLS
    total = rows_n * cols_n
    spots = total - 2 * rows_n
    shuffled = jax.random.permutation(key, spots).astype(jnp.int32)
    land_pos = (shuffled[:LAND] + 2 * rows_n).astype(jnp.int32)
    land = jnp.zeros((total,), jnp.int32).at[land_pos].set(1)
    ranks = (jnp.cumsum(1 - land) - 1).astype(jnp.int32)
    curve = jnp.arange(total, dtype=jnp.int32)
    column = curve // rows_n
    within = curve % rows_n
    row_no = jnp.where(column % 2 == 0, within, rows_n - 1 - within)
    moves = ((-1, 0), (1, 0), (0, -1), (0, 1), (-1, -1), (-1, 1), (1, -1), (1, 1))
    listed = []
    for move_row, move_col in moves:
        next_row = row_no + move_row
        next_col = column + move_col
        inside = (next_row >= 0) & (next_row < rows_n) & (next_col >= 0) & (next_col < cols_n)
        safe_row = jnp.clip(next_row, 0, rows_n - 1)
        safe_col = jnp.clip(next_col, 0, cols_n - 1)
        position = (safe_col * rows_n + jnp.where(safe_col % 2 == 0, safe_row, rows_n - 1 - safe_row)).astype(jnp.int32)
        usable = inside & (land[position] == 0)
        listed.append(jnp.where(usable, ranks[position], -1).astype(jnp.int32))
    table = jnp.stack(listed, 1)
    picked = jnp.argsort(land * total + curve, stable=True)[:TILES].astype(jnp.int32)
    return table[picked].astype(jnp.int32)


def levels(own_key, shape, cuts, smallest, top_value):
    level, own = 1.0, jax.random.fold_in(own_key, 6)
    for dim, blocks in cuts:
        draws = jnp.exp(jax.random.uniform(jax.random.fold_in(own, dim), (blocks,), jnp.float32, smallest / len(cuts), top_value / len(cuts)))
        level = level * jnp.repeat(draws, shape[dim] // blocks).reshape([-1 if axis == dim else 1 for axis in range(len(shape))])
    return level


def bell_draw(own_key, dims, scale, bound, shards=(), held_as=jnp.bfloat16):
    values = scale * jax.random.normal(own_key, dims, jnp.float32)
    if shards:
        values = values * levels(own_key, dims, shards, -0.22, 0.18)
    return jnp.clip(values, -bound, bound).astype(held_as)


def setup_inputs(seed: int = 0, part: int = 0) -> dict:
    streams_of = jax.random.split(jax.random.key(seed), 6)
    part_splits = jax.random.split(jax.random.fold_in(streams_of[5], part), 6)
    ocean_state = bell_draw(part_splits[0], (TILES, TH, TW, LC), 1.0, 6.0, ((0, 16),))
    cotangent = bell_draw(part_splits[1], (TILES, TH, TW, LC), 1.0, 6.0, ((0, 16),))
    first_kernel = bell_draw(streams_of[2], (3, 3, C, LC), (9 * C) ** -0.5, 0.375)
    second_kernel = bell_draw(streams_of[3], (3, 3, C, LC), (9 * C) ** -0.5, 0.375)
    neighbours = draw_neighbours(jax.random.fold_in(streams_of[5], 71), part)
    return dict(ocean_state=ocean_state, cotangent=cotangent, first_kernel=first_kernel, second_kernel=second_kernel, neighbours=neighbours)


cycle_sources = ((0, 1), (0, 0), (1, 1), (1, 0), (2, 3), (2, 2), (2, 1), (2, 0))

def gelu_tanh(values):
    return jax.nn.gelu(values, approximate=True)

def tile_rims(field):
    edge_rows = jnp.stack([field[:, 0], field[:, -1]], 1)
    edge_columns = jnp.stack([field[:, :, 0], field[:, :, -1]], 1)
    corners = jnp.stack([field[:, 0, 0], field[:, 0, -1], field[:, -1, 0], field[:, -1, -1]], 1)
    return (edge_rows, edge_columns, corners)

def cycle_pieces(rims, tile_links):
    pieces = []
    for direction in range(8):
        member, part_no = cycle_sources[direction]
        target = tile_links[direction]
        piece = rims[member][jnp.maximum(target, 0).astype(jnp.int32), part_no]
        pieces.append(jnp.where(target >= 0, piece, jnp.zeros_like(piece)))
    return pieces

def assemble(own_tile, pieces):
    above_row, below_row, left_col, right_col, upper_left, upper_right, lower_left, lower_right = pieces
    top_line = jnp.concatenate([upper_left[None], above_row, upper_right[None]], 0)
    bottom_line = jnp.concatenate([lower_left[None], below_row, lower_right[None]], 0)
    middle = jnp.concatenate([left_col[:, None], own_tile, right_col[:, None]], 1)
    return jnp.concatenate([top_line[None], middle, bottom_line[None]], 0)

def grouped(padded, kernel):
    groups_n = kernel.shape[3] // kernel.shape[2]
    result = lax.conv_general_dilated(padded[None], kernel, (1, 1), 'VALID', dimension_numbers=('NHWC', 'HWIO', 'NHWC'), feature_group_count=groups_n, preferred_element_type=jnp.float32)
    return result[0]

def flipped(kernel):
    width = kernel.shape[2]
    levels_n = kernel.shape[3] // width
    mirror = kernel[::-1, ::-1].reshape(3, 3, width, levels_n, width)
    return mirror.transpose(0, 1, 4, 3, 2).reshape(3, 3, width, levels_n * width)

def weight_grad(padded, cot_tile, width):
    rows_n, cols_n = (cot_tile.shape[0], cot_tile.shape[1])
    grads = cot_tile.reshape(rows_n, cols_n, -1, width).astype(jnp.float32)
    lines = []
    for shift_y in range(3):
        entries = []
        for shift_x in range(3):
            window = padded[shift_y:shift_y + rows_n, shift_x:shift_x + cols_n].reshape(rows_n, cols_n, -1, width).astype(jnp.float32)
            product = jnp.einsum('hwli,hwlo->lio', window, grads)
            entries.append(product.transpose(1, 0, 2).reshape(width, -1))
        lines.append(jnp.stack(entries))
    return jnp.stack(lines)

def reference(ocean_state, cotangent, first_kernel, second_kernel, neighbours):
    tile_ids = jnp.arange(TILES, dtype=jnp.int32)
    width = C
    state_rims = tile_rims(ocean_state)
    cot_rims = tile_rims(cotangent)

    def pad_of(field, rims, tile_no):
        return assemble(field[tile_no], cycle_pieces(rims, neighbours[tile_no]))

    def forward(tile_no):
        return gelu_tanh(grouped(pad_of(ocean_state, state_rims, tile_no), first_kernel)).astype(jnp.bfloat16)
    hidden = lax.map(forward, tile_ids)
    hidden_rims = tile_rims(hidden)
    first_flip = flipped(first_kernel)
    second_flip = flipped(second_kernel)

    def backward(tile_no):
        pre = grouped(pad_of(ocean_state, state_rims, tile_no), first_kernel)
        back_hidden = grouped(pad_of(cotangent, cot_rims, tile_no), second_flip)
        pullback = jax.vjp(gelu_tanh, pre)[1]
        pre_grad = pullback(back_hidden)[0].astype(jnp.bfloat16)
        second_part = weight_grad(pad_of(hidden, hidden_rims, tile_no), cotangent[tile_no], width)
        return (pre_grad, second_part)
    pre_grad, second_parts = lax.map(backward, tile_ids)
    grad_rims = tile_rims(pre_grad)

    def adjoint(tile_no):
        back_state = grouped(pad_of(pre_grad, grad_rims, tile_no), first_flip)
        state_tile = (cotangent[tile_no].astype(jnp.float32) + back_state).astype(jnp.bfloat16)
        first_part = weight_grad(pad_of(ocean_state, state_rims, tile_no), pre_grad[tile_no], width)
        return (state_tile, first_part)
    state_grad, first_parts = lax.map(adjoint, tile_ids)
    scale = 1.0 / math.sqrt(TILES * TH * TW)
    return (state_grad, lax.optimization_barrier(jnp.sum(first_parts, 0)) * scale, lax.optimization_barrier(jnp.sum(second_parts, 0)) * scale)
```

```python
import functools
import math

import jax
import jax.numpy as jnp
from jax import lax
from jax.experimental import pallas as pl
from jax.experimental.pallas import tpu as pltpu
from jax.sharding import PartitionSpec as P

CUBE = 0.044715
ROOT = math.sqrt(2.0 / math.pi)
VMEM_LIMIT = 56 * 1024 * 1024
SMEM = pl.BlockSpec(memory_space=pltpu.SMEM)
VMEM = pl.BlockSpec(memory_space=pltpu.VMEM)


def shape_of(dims, dtype):
    return jax.ShapeDtypeStruct(dims, dtype)


def partners(me):
    odd = lax.rem(me, 2)
    return me + 1 - 2 * odd, me - 1 + 2 * odd


def gelu_pair(v):
    square = v * v
    t = jnp.tanh(ROOT * v * (1.0 + CUBE * square))
    half = 0.5 * (1.0 + t)
    slope = half + (0.5 * ROOT) * v * (1.0 - t * t) * (1.0 + (3.0 * CUBE) * square)
    return v * half, slope


def pack_kernel(tiles, links, me_ref, *refs):
    blocks, (send, own, on_out, off_out) = refs[:8], refs[8:]
    me = me_ref[0]
    sides = ([], [])
    for f in range(2):
        top, bottom, left, right = blocks[4 * f : 4 * f + 4]
        width = right.shape[1]
        for side, block, first in ((0, left, 0), (1, right, width - 2)):
            values = block[...].astype(jnp.float32)
            pair = jnp.stack([values[:, first + c, :] for c in range(2)], 0).astype(jnp.bfloat16)
            own[side, f] = pair
            sides[side].append(pair)
    left_pair, right_pair = (jnp.stack(side, 0) for side in sides)

    def fill(j, carry):
        send[j] = jnp.where(j > me, right_pair, left_pair)
        return carry

    lax.fori_loop(0, tiles, fill, 0)
    for target, out in zip(partners(me), (on_out, off_out)):
        for f in range(2):
            top, bottom = blocks[4 * f][...], blocks[4 * f + 1][...]
            rows = jnp.where(links[0, 1] == target, bottom, jnp.zeros_like(bottom))
            out[f] = jnp.where(links[0, 0] == target, top, rows)


def pack(tiles, links, me, state, cot):
    rows_n, cols_n, chans = state.shape
    specs = [
        pl.BlockSpec((2, cols_n, chans), lambda i: (0, 0, 0)),
        pl.BlockSpec((2, cols_n, chans), lambda i: (rows_n // 2 - 1, 0, 0)),
        pl.BlockSpec((rows_n, 16, chans), lambda i: (0, 0, 0)),
        pl.BlockSpec((rows_n, 16, chans), lambda i: (0, cols_n // 16 - 1, 0)),
    ]
    return pl.pallas_call(
        functools.partial(pack_kernel, tiles),
        grid=(1,),
        in_specs=[SMEM, SMEM] + specs * 2,
        out_specs=[VMEM] * 4,
        out_shape=[
            shape_of((tiles, 2, 2, rows_n, chans), jnp.bfloat16),
            shape_of((2, 2, 2, rows_n, chans), jnp.bfloat16),
            shape_of((2, 2, cols_n, chans), jnp.bfloat16),
            shape_of((2, 2, cols_n, chans), jnp.bfloat16),
        ],
        compiler_params=pltpu.CompilerParams(vmem_limit_bytes=VMEM_LIMIT),
        name="pack",
    )(links, me, *([state] * 4), *([cot] * 4))


def halo_rows(links, me, on_in, off_in, f):
    found = []
    for link in (0, 1):
        rows = jnp.zeros(on_in.shape[1:], on_in.dtype)
        for source, packet in zip(partners(me), (on_in, off_in)):
            rows = jnp.where(links[0, link] == source, packet[f], rows)
        found.append(rows)
    return found


def same_level(width, chans):
    down = lax.broadcasted_iota(jnp.int32, (chans, chans), 0) // width
    across = lax.broadcasted_iota(jnp.int32, (chans, chans), 1) // width
    return down == across


def diagonal(product, mask, width):
    kept = jnp.where(mask, product, 0.0)
    return sum(kept[at : at + width] for at in range(0, product.shape[0], width))


def thirds(ref, row, values):
    count, cols_n, chans = values.shape
    flat = values.reshape(count * cols_n, chans).astype(jnp.float32)
    left = pltpu.roll(flat, 1, 0).astype(ref.dtype).reshape(values.shape)
    right = pltpu.roll(flat, count * cols_n - 1, 0).astype(ref.dtype).reshape(values.shape)
    ref[pl.ds(row, count), :, 0:chans] = left
    ref[pl.ds(row, count), :, chans : 2 * chans] = values
    ref[pl.ds(row, count), :, 2 * chans : 3 * chans] = right


def windows(ref, starts, count):
    parts = []
    for start in starts:
        rows = ref[pl.ds(start, count)]
        parts.append(rows.reshape(rows.shape[0] * rows.shape[1], rows.shape[2]))
    return jnp.concatenate(parts, 1)


def dot(a, b):
    return jnp.dot(a, b, preferred_element_type=jnp.float32)


def main_kernel(
    chunk, links, me_ref, state, cot, on_in, off_in, first_k, second_k,
    grad, first_acc, second_acc, w_pre, w_back, w_state, s3, c3, acc1, acc2,
):
    me = me_ref[0]
    rows_n, cols_n, chans = state.shape
    width = first_k.shape[2]
    mask = same_level(width, chans)
    for tap in range(9):
        for kernel, plain, turned in ((first_k, w_pre, w_state), (second_k, None, w_back)):
            block = kernel[tap // 3, tap % 3].astype(jnp.float32)
            dense = jnp.where(mask, jnp.concatenate([block] * (chans // width), 0), 0.0)
            if plain is not None:
                plain[pl.ds(tap * chans, chans)] = dense.astype(jnp.bfloat16)
            turned[pl.ds((8 - tap) * chans, chans)] = dense.T.astype(jnp.bfloat16)
    for f, (field, store) in enumerate(((state, s3), (cot, c3))):
        above, below = halo_rows(links, me, on_in, off_in, f)
        thirds(store, 0, above)
        thirds(store, rows_n + 2, below)

        def spread(i, carry, field=field, store=store):
            row = i * chunk
            thirds(store, row + 2, field[pl.ds(row, chunk)])
            return carry

        lax.fori_loop(0, rows_n // chunk, spread, 0)

    def fields(starts, count):
        near_state, near_cot = windows(s3, starts, count), windows(c3, starts, count)
        hidden, slope = gelu_pair(dot(near_state, w_pre[...]))
        return near_state, near_cot, hidden, dot(near_cot, w_back[...]) * slope

    x = lax.rem(lax.broadcasted_iota(jnp.int32, (chunk * cols_n, chans), 0), cols_n)
    inner = (x > 0) & (x < cols_n - 1)
    acc1[...] = jnp.zeros_like(acc1)
    acc2[...] = jnp.zeros_like(acc2)

    def step(i, carry):
        row = i * chunk
        near_state, near_cot, hidden, grads = fields([row + 1 + a for a in range(3)], chunk)
        grads = jnp.where(inner, grads, 0.0).astype(jnp.bfloat16)
        hidden = jnp.where(inner, hidden, 0.0).astype(jnp.bfloat16)
        grad[pl.ds(row + 1, chunk)] = grads.reshape(chunk, cols_n, chans)
        acc1[...] += dot(grads.T, near_state)
        acc2[...] += dot(hidden.T, near_cot)
        return carry

    lax.fori_loop(0, rows_n // chunk, step, 0)
    for link, row, at in ((0, 0, 0), (1, rows_n + 1, rows_n + 1)):
        grads = fields([row + a for a in range(3)], 1)[3]
        grads = jnp.where(links[0, link] >= 0, grads, 0.0)
        grad[at] = grads.astype(jnp.bfloat16)
    for tap in range(9):
        part = slice(tap * chans, (tap + 1) * chans)
        first_acc[tap] = diagonal(acc1[:, part].T, mask, width)
        second_acc[8 - tap] = diagonal(acc2[:, part], mask, width)


def main_part(links, me, state, cot, on_in, off_in, first_k, second_k):
    rows_n, cols_n, chans = state.shape
    width = first_k.shape[2]
    chunk = 4
    flops = 2 * rows_n * cols_n * 9 * chans * chans * 4
    return pl.pallas_call(
        functools.partial(main_kernel, chunk),
        in_specs=[SMEM, SMEM] + [VMEM] * 6,
        out_specs=[VMEM] * 6,
        out_shape=[
            shape_of((rows_n + 2, cols_n, chans), jnp.bfloat16),
            shape_of((9, width, chans), jnp.float32),
            shape_of((9, width, chans), jnp.float32),
            shape_of((9 * chans, chans), jnp.bfloat16),
            shape_of((9 * chans, chans), jnp.bfloat16),
            shape_of((9 * chans, chans), jnp.bfloat16),
        ],
        scratch_shapes=[
            pltpu.VMEM((rows_n + 4, cols_n, 3 * chans), jnp.bfloat16),
            pltpu.VMEM((rows_n + 4, cols_n, 3 * chans), jnp.bfloat16),
            pltpu.VMEM((chans, 9 * chans), jnp.float32),
            pltpu.VMEM((chans, 9 * chans), jnp.float32),
        ],
        compiler_params=pltpu.CompilerParams(vmem_limit_bytes=VMEM_LIMIT),
        cost_estimate=pl.CostEstimate(flops=flops, bytes_accessed=5 << 20, transcendentals=1 << 19),
        name="main",
    )(links, me, state, cot, on_in, off_in, first_k, second_k)


BASE = 16


def edge_kernel(
    links, me_ref, own, received, on_in, off_in, w_pre, w_back, first_acc, second_acc,
    keep, pass_on, edge_grad, store, lhs_s, lhs_c,
):
    me = me_ref[0]
    rows_n, chans = own.shape[3], own.shape[4]
    cols_n = on_in.shape[2]
    width = first_acc.shape[1]
    span = rows_n + 16
    store[...] = jnp.zeros_like(store)
    low, high = pl.ds(BASE - 2, 2), pl.ds(BASE + rows_n, 2)
    for f in range(2):
        rows = halo_rows(links, me, on_in, off_in, f)
        for side, link, over, under in ((0, 2, 4, 6), (1, 3, 5, 7)):
            outer, mine = (0, 2) if side == 0 else (6, 4)

            def sent(entry):
                tile = links[0, entry]
                piece = received[jnp.maximum(tile, 0), f].astype(jnp.float32)
                return jnp.where(tile >= 0, piece, 0.0)

            beside, corner_over, corner_under = sent(link), sent(over), sent(under)
            for c in range(2):
                store[f, mine + c, pl.ds(BASE, rows_n)] = own[side, f, c].astype(jnp.float32)
                store[f, outer + c, pl.ds(BASE, rows_n)] = beside[c]
                store[f, outer + c, low] = corner_over[c, rows_n - 2 : rows_n]
                store[f, outer + c, high] = corner_under[c, 0:2]
            at = 0 if side == 0 else cols_n - 16
            first = 0 if side == 0 else 14
            for where, halo in ((BASE - 2, rows[0]), (BASE + rows_n, rows[1])):
                edge = halo[:, at : at + 16].astype(jnp.float32)
                for r in range(2):
                    for c in range(2):
                        store[f, mine + c, pl.ds(where + r, 1)] = edge[r, first + c : first + c + 1]
        target = (lhs_s, lhs_c)[f]
        for column, base in enumerate((0, 1, 4, 5)):
            for a in range(3):
                for b in range(3):
                    lanes = pl.ds((3 * a + b) * chans, chans)
                    column_in = store.at[f, base + b]
                    target[pl.ds(column * span, rows_n), lanes] = column_in[
                        pl.ds(BASE - 1 + a, rows_n)
                    ].astype(jnp.bfloat16)
                    ends = [column_in[pl.ds(BASE - 2 + a, 8)], column_in[pl.ds(BASE + rows_n - 1 + a, 8)]]
                    target[pl.ds(column * span + rows_n, 16), lanes] = jnp.concatenate(ends, 0).astype(
                        jnp.bfloat16
                    )
    hidden, slope = gelu_pair(dot(lhs_s[...], w_pre[...]))
    grads = dot(lhs_c[...], w_back[...]) * slope
    valid = ((2, 4, 6), (None, 0, 1), (None, 0, 1), (3, 5, 7))
    for column in range(4):
        spans = ((0, rows_n), (rows_n, 8), (rows_n + 8, 8))
        for entry, (start, count) in zip(valid[column], spans):
            start += column * span
            piece = grads[start : start + count]
            if entry is not None:
                piece = jnp.where(links[0, entry] >= 0, piece, 0.0)
            edge_grad[pl.ds(start, count)] = piece.astype(jnp.bfloat16).astype(jnp.float32)

    def inner(values):
        return jnp.concatenate([values[span : span + rows_n], values[2 * span : 2 * span + rows_n]], 0)

    def inner_of(ref):
        return jnp.concatenate([ref[pl.ds(span, rows_n)], ref[pl.ds(2 * span, rows_n)]], 0)

    def over_cells(a, b):
        return lax.dot_general(a, b, (((0,), (0,)), ((), ())), preferred_element_type=jnp.float32)

    mask = same_level(width, chans)
    first_p = over_cells(inner_of(lhs_s), inner(grads).astype(jnp.bfloat16))
    second_p = over_cells(inner(hidden).astype(jnp.bfloat16), inner_of(lhs_c))
    even = lax.rem(me, 2) == 0
    for tap in range(9):
        part = slice(tap * chans, (tap + 1) * chans)
        first = first_acc[tap] + diagonal(first_p[part], mask, width)
        turned = slice((8 - tap) * chans, (9 - tap) * chans)
        second = second_acc[tap] + diagonal(second_p[:, turned], mask, width)
        keep[tap] = jnp.where(even, first, second)
        pass_on[tap] = jnp.where(even, second, first)


def edge_part(links, me, own, received, on_in, off_in, w_pre, w_back, first_acc, second_acc):
    rows_n, chans = own.shape[3:]
    cells = 4 * (rows_n + 16)
    return pl.pallas_call(
        edge_kernel,
        in_specs=[SMEM, SMEM] + [VMEM] * 8,
        out_specs=[VMEM] * 3,
        out_shape=[
            shape_of(first_acc.shape, jnp.float32),
            shape_of(first_acc.shape, jnp.float32),
            shape_of((cells, chans), jnp.float32),
        ],
        scratch_shapes=[
            pltpu.VMEM((2, 8, rows_n + 32, chans), jnp.float32),
            pltpu.VMEM((cells, 9 * chans), jnp.bfloat16),
            pltpu.VMEM((cells, 9 * chans), jnp.bfloat16),
        ],
        compiler_params=pltpu.CompilerParams(vmem_limit_bytes=VMEM_LIMIT),
        cost_estimate=pl.CostEstimate(flops=200 << 20, bytes_accessed=3 << 20, transcendentals=1 << 15),
        name="edge",
    )(links, me, own, received, on_in, off_in, w_pre, w_back, first_acc, second_acc)


def state_kernel(chunk, grad, edge_grad, w_state, cot, out, g3):
    rows_n, cols_n, chans = cot.shape
    span = rows_n + 16
    x = lax.broadcasted_iota(jnp.int32, (cols_n, chans), 0)
    at_left, at_right = x == 0, x == cols_n - 1

    def place(row, at):
        def column(number):
            return edge_grad[pl.ds(number * span + at, 1)]

        values = grad[row].astype(jnp.float32)
        values = jnp.where(at_left, column(1), jnp.where(at_right, column(2), values))
        left = jnp.where(at_left, column(0), pltpu.roll(values, 1, 0))
        right = jnp.where(at_right, column(3), pltpu.roll(values, cols_n - 1, 0))
        g3[row, :, 0:chans] = left.astype(g3.dtype)
        g3[row, :, chans : 2 * chans] = values.astype(g3.dtype)
        g3[row, :, 2 * chans : 3 * chans] = right.astype(g3.dtype)

    def spread(i, carry):
        for r in range(chunk):
            place(i * chunk + r + 1, i * chunk + r)
        return carry

    lax.fori_loop(0, rows_n // chunk, spread, 0)
    place(0, rows_n)
    place(rows_n + 1, rows_n + 8)

    def step(i, carry):
        row = i * chunk
        back = dot(windows(g3, [row + a for a in range(3)], chunk), w_state[...])
        own = cot[pl.ds(row, chunk)].astype(jnp.float32)
        out[pl.ds(row, chunk)] = (own + back.reshape(own.shape)).astype(out.dtype)
        return carry

    lax.fori_loop(0, rows_n // chunk, step, 0)


def state_part(grad, edge_grad, w_state, cot):
    rows_n, cols_n, chans = cot.shape
    return pl.pallas_call(
        functools.partial(state_kernel, 4),
        in_specs=[VMEM] * 4,
        out_specs=VMEM,
        out_shape=shape_of(cot.shape, jnp.bfloat16),
        scratch_shapes=[pltpu.VMEM((rows_n + 2, cols_n, 3 * chans), jnp.bfloat16)],
        compiler_params=pltpu.CompilerParams(vmem_limit_bytes=VMEM_LIMIT),
        cost_estimate=pl.CostEstimate(flops=1200 << 20, bytes_accessed=3 << 20, transcendentals=0),
        name="state",
    )(grad, edge_grad, w_state, cot)


def exchanged(value, tiles, pairs):
    both = [(a, b) for a, b in pairs if a < tiles and b < tiles]
    return lax.ppermute(value, "tiles", both + [(b, a) for a, b in both])


def summed(keep, pass_on, me, tiles, scale):
    even = lax.rem(me, 2) == 0
    if tiles & (tiles - 1):
        first, second = jnp.where(even, keep, pass_on), jnp.where(even, pass_on, keep)
        first, second = lax.psum((first, second), "tiles")
        return first * scale, second * scale
    on_chip = [(t, t + 1) for t in range(0, tiles, 2)]
    total = keep + exchanged(pass_on, tiles, on_chip)
    distance = 2
    while distance < tiles:
        pairs = [(t, t + distance) for t in range(tiles) if not t & distance]
        total = total + exchanged(total, tiles, pairs)
        distance *= 2
    total = total * scale
    other = exchanged(total, tiles, on_chip)
    return jnp.where(even, total, other), jnp.where(even, other, total)


def local(ocean_state, cotangent, first_kernel, second_kernel, neighbours):
    state, cot = ocean_state[0], cotangent[0]
    rows_n, cols_n, chans = state.shape
    tiles = lax.axis_size("tiles")
    index = lax.axis_index("tiles")
    me = jnp.reshape(index, (1,)).astype(jnp.int32)
    send, own, on_out, off_out = pack(tiles, neighbours, me, state, cot)
    received = lax.all_to_all(send, "tiles", 0, 0)
    on_in = exchanged(on_out, tiles, [(t, t + 1) for t in range(0, tiles, 2)])
    off_in = exchanged(off_out, tiles, [(t, t + 1) for t in range(1, tiles, 2)])
    grad, first_acc, second_acc, w_pre, w_back, w_state = main_part(
        neighbours, me, state, cot, on_in, off_in, first_kernel, second_kernel
    )
    keep, pass_on, edge_grad = edge_part(
        neighbours, me, own, received, on_in, off_in, w_pre, w_back, first_acc, second_acc
    )
    state_grad = state_part(grad, edge_grad, w_state, cot)
    scale = 1.0 / math.sqrt(tiles * rows_n * cols_n)
    first, second = summed(keep, pass_on, index, tiles, scale)
    shape = first_kernel.shape
    return state_grad[None], first.reshape(shape), second.reshape(shape)


def solution(mesh):
    placed = (
        P(("groups", "tiles"), None, None, None),
        P(("groups", "tiles"), None, None, None),
        P(),
        P(),
        P("tiles", None),
    )
    return jax.shard_map(
        local,
        mesh=mesh,
        in_specs=placed,
        out_specs=(
            P(("groups", "tiles"), None, None, None),
            P("groups", None, None, None),
            P("groups", None, None, None),
        ),
        check_vma=False,
    )
```

```python
import functools
import math

import jax
import jax.numpy as jnp
from jax import lax
from jax.experimental import pallas as pl
from jax.experimental.pallas import tpu as pltpu
from jax.sharding import PartitionSpec as P

CUBE = 0.044715
ROOT = math.sqrt(2.0 / math.pi)
MIB = 1 << 20
SMEM = pl.BlockSpec(memory_space=pltpu.SMEM)
VMEM = pl.BlockSpec(memory_space=pltpu.VMEM)


def shape_of(dims, dtype):
    return jax.ShapeDtypeStruct(dims, dtype)


def partners(me):
    odd = lax.rem(me, 2)
    return me + 1 - 2 * odd, me - 1 + 2 * odd


def gelu_pair(v):
    square = v * v
    t = jnp.tanh(ROOT * v * (1.0 + CUBE * square))
    half = 0.5 * (1.0 + t)
    slope = half + (0.5 * ROOT) * v * (1.0 - t * t) * (1.0 + (3.0 * CUBE) * square)
    return v * half, slope


def row_kernel(links, me_ref, *refs):
    blocks, outs = refs[:4], refs[4:]
    for target, out in zip(partners(me_ref[0]), outs):
        for f in range(2):
            top, bottom = blocks[2 * f][...], blocks[2 * f + 1][...]
            rows = jnp.where(links[0, 1] == target, bottom, jnp.zeros_like(bottom))
            out[f] = jnp.where(links[0, 0] == target, top, rows)


def pack_rows(links, me, state, cot):
    rows_n, cols_n, chans = state.shape
    specs = [
        pl.BlockSpec((2, cols_n, chans), lambda i: (0, 0, 0)),
        pl.BlockSpec((2, cols_n, chans), lambda i: (rows_n // 2 - 1, 0, 0)),
    ]
    return pl.pallas_call(
        row_kernel,
        grid=(1,),
        in_specs=[SMEM, SMEM] + specs * 2,
        out_specs=[VMEM] * 2,
        out_shape=[shape_of((2, 2, cols_n, chans), jnp.bfloat16)] * 2,
        compiler_params=pltpu.CompilerParams(vmem_limit_bytes=60 * MIB),
        name="pack_rows",
    )(links, me, *([state] * 2), *([cot] * 2))


def column_kernel(tiles, me_ref, after, *refs):
    blocks, (send, own) = refs[:4], refs[4:]
    me = me_ref[0]
    for f in range(2):
        for side, first in ((0, 0), (1, 14)):
            values = blocks[2 * f + side][...].astype(jnp.float32)
            for c in range(2):
                own[side, f, c] = values[:, first + c, :].astype(jnp.bfloat16)
    left, right = own[0], own[1]

    def fill(j, carry):
        send[j] = jnp.where(j > me, right, left)
        return carry

    lax.fori_loop(0, tiles, fill, 0)


def pack_columns(tiles, me, after, state, cot):
    rows_n, cols_n, chans = state.shape
    specs = [
        pl.BlockSpec((rows_n, 16, chans), lambda i: (0, 0, 0)),
        pl.BlockSpec((rows_n, 16, chans), lambda i: (0, cols_n // 16 - 1, 0)),
    ]
    return pl.pallas_call(
        functools.partial(column_kernel, tiles),
        grid=(1,),
        in_specs=[SMEM, pl.BlockSpec(memory_space=pl.ANY)] + specs * 2,
        out_specs=[VMEM] * 2,
        out_shape=[
            shape_of((tiles, 2, 2, rows_n, chans), jnp.bfloat16),
            shape_of((2, 2, 2, rows_n, chans), jnp.bfloat16),
        ],
        compiler_params=pltpu.CompilerParams(vmem_limit_bytes=60 * MIB),
        name="pack_columns",
    )(me, after, *([state] * 2), *([cot] * 2))


def halo_rows(links, me, on_in, off_in, f):
    found = []
    for link in (0, 1):
        rows = jnp.zeros(on_in.shape[1:], on_in.dtype)
        for source, packet in zip(partners(me), (on_in, off_in)):
            rows = jnp.where(links[0, link] == source, packet[f], rows)
        found.append(rows)
    return found


def same_level(width, chans):
    down = lax.broadcasted_iota(jnp.int32, (chans, chans), 0) // width
    across = lax.broadcasted_iota(jnp.int32, (chans, chans), 1) // width
    return down == across


def diagonal(product, mask, width):
    kept = jnp.where(mask, product, 0.0)
    return sum(kept[at : at + width] for at in range(0, product.shape[0], width))


def thirds(ref, row, values):
    count, cols_n, chans = values.shape
    flat = values.reshape(count * cols_n, chans).astype(jnp.float32)
    left = pltpu.roll(flat, 1, 0).astype(ref.dtype)
    right = pltpu.roll(flat, count * cols_n - 1, 0).astype(ref.dtype)
    for part, piece in enumerate((left, values, right)):
        lanes = slice(part * chans, (part + 1) * chans)
        ref[pl.ds(row // 2, count // 2), :, :, lanes] = piece.reshape(count // 2, 2, cols_n, chans)


def windows(ref, pair, count):
    parts = []
    for row in range(4):
        rows = ref[pl.ds(pair + row // 2, count), row % 2]
        parts.append(rows.reshape(count * rows.shape[1], rows.shape[2]))
    return jnp.concatenate(parts, 1)


def dot(a, b):
    return jnp.dot(a, b, preferred_element_type=jnp.float32)


def spans_of(total, most):
    count = pl.cdiv(total, most)
    bounds = [total * i // count for i in range(count + 1)]
    return [(lo, hi - lo) for lo, hi in zip(bounds, bounds[1:])]


def level_blocks(kernel, tap, mask):
    block = kernel[tap // 3, tap % 3].astype(jnp.float32)
    return jnp.where(mask, jnp.concatenate([block] * (mask.shape[0] // block.shape[0]), 0), 0.0)


def fill_paired(ref, kernel, mask, turned):
    chans = mask.shape[0]
    none = jnp.zeros((3 * chans, chans), ref.dtype)
    ref[9 * chans : 12 * chans, 0:chans] = none
    ref[0 : 3 * chans, chans : 2 * chans] = none
    for tap in range(9):
        dense = level_blocks(kernel, tap, mask)
        if turned:
            paired(ref, 8 - tap, dense.T.astype(ref.dtype))
        else:
            paired(ref, tap, dense.astype(ref.dtype))


def paired(ref, tap, dense):
    chans = dense.shape[0]
    for row in range(2):
        ref[pl.ds((tap + 3 * row) * chans, chans), row * chans : (row + 1) * chans] = dense


def main_kernel(
    links, me_ref, state, cot, on_in, off_in, first_k, second_k,
    grad, first_acc, second_acc, w_pre, w_back, s3, c3, acc1, acc2,
):
    me = me_ref[0]
    rows_n, cols_n, chans = state.shape
    width = first_k.shape[2]
    mask = same_level(width, chans)
    fill_paired(w_pre, first_k, mask, False)
    fill_paired(w_back, second_k, mask, True)
    for f, (field, store) in enumerate(((state, s3), (cot, c3))):
        above, below = halo_rows(links, me, on_in, off_in, f)
        thirds(store, 0, above)
        thirds(store, rows_n + 2, below)
        for row, count in spans_of(rows_n // 2, 4):
            thirds(store, 2 * row + 2, field[pl.ds(2 * row, 2 * count)])

    acc1[...] = jnp.zeros_like(acc1)
    acc2[...] = jnp.zeros_like(acc2)
    pairs_n = rows_n // 2 + 1
    for pair, count in spans_of(pairs_n, PAIRS):
        near_state, near_cot = windows(s3, pair, count), windows(c3, pair, count)
        hidden, slope = gelu_pair(dot(near_state, w_pre[...]))
        grads = dot(near_cot, w_back[...]) * slope
        cell = lax.broadcasted_iota(jnp.int32, grads.shape, 0)
        lane = lax.broadcasted_iota(jnp.int32, grads.shape, 1)
        x = lax.rem(cell, cols_n)
        inner = (x > 0) & (x < cols_n - 1)
        if pair == 0:
            outside = (cell < cols_n) & (lane < chans)
            inner = inner & ~outside
            grads = jnp.where(outside & (links[0, 0] < 0), 0.0, grads)
        if pair + count == pairs_n:
            outside = (cell >= (count - 1) * cols_n) & (lane >= chans)
            inner = inner & ~outside
            grads = jnp.where(outside & (links[0, 1] < 0), 0.0, grads)
        for row in range(2):
            piece = grads[:, row * chans : (row + 1) * chans].astype(jnp.bfloat16)
            grad[pl.ds(pair, count), row] = piece.reshape(count, cols_n, chans)
        grads = jnp.where(inner, grads, 0.0).astype(jnp.bfloat16)
        hidden = jnp.where(inner, hidden, 0.0).astype(jnp.bfloat16)
        acc1[...] += dot(grads.T, near_state)
        acc2[...] += dot(hidden.T, near_cot)
    for tap in range(9):
        one, two = (slice((tap + 3 * r) * chans, (tap + 3 * r + 1) * chans) for r in range(2))
        first = acc1[0:chans, one] + acc1[chans : 2 * chans, two]
        second = acc2[0:chans, one] + acc2[chans : 2 * chans, two]
        first_acc[tap] = diagonal(first.T, mask, width)
        second_acc[8 - tap] = diagonal(second, mask, width)


PAIRS = 9


def main_part(links, me, state, cot, on_in, off_in, first_k, second_k):
    rows_n, cols_n, chans = state.shape
    width = first_k.shape[2]
    flops = 2 * rows_n * cols_n * 9 * chans * chans * 4
    return pl.pallas_call(
        main_kernel,
        in_specs=[SMEM, SMEM] + [VMEM] * 6,
        out_specs=[VMEM] * 3,
        out_shape=[
            shape_of((rows_n // 2 + 1, 2, cols_n, chans), jnp.bfloat16),
            shape_of((9, width, chans), jnp.float32),
            shape_of((9, width, chans), jnp.float32),
        ],
        scratch_shapes=[
            pltpu.VMEM((12 * chans, 2 * chans), jnp.bfloat16),
            pltpu.VMEM((12 * chans, 2 * chans), jnp.bfloat16),
            pltpu.VMEM((rows_n // 2 + 2, 2, cols_n, 3 * chans), jnp.bfloat16),
            pltpu.VMEM((rows_n // 2 + 2, 2, cols_n, 3 * chans), jnp.bfloat16),
            pltpu.VMEM((2 * chans, 12 * chans), jnp.float32),
            pltpu.VMEM((2 * chans, 12 * chans), jnp.float32),
        ],
        compiler_params=pltpu.CompilerParams(vmem_limit_bytes=24 * MIB),
        cost_estimate=pl.CostEstimate(flops=20 * flops, bytes_accessed=5 << 20, transcendentals=1 << 19),
        name="main",
    )(links, me, state, cot, on_in, off_in, first_k, second_k)


BASE = 16


def edge_kernel(
    links, me_ref, own, received, on_in, off_in, first_k, second_k, first_acc, second_acc,
    keep, pass_on, edge_grad, store, lhs_s, lhs_c, w_pre, w_back,
):
    me = me_ref[0]
    rows_n, chans = own.shape[3], own.shape[4]
    cols_n = on_in.shape[2]
    width = first_acc.shape[1]
    span = rows_n + 16
    mask = same_level(width, chans)
    for tap in range(9):
        at = slice(tap * chans, (tap + 1) * chans)
        w_pre[at] = level_blocks(first_k, tap, mask).astype(w_pre.dtype)
        w_back[at] = level_blocks(second_k, 8 - tap, mask).T.astype(w_back.dtype)
    store[...] = jnp.zeros_like(store)
    low, high = pl.ds(BASE - 2, 2), pl.ds(BASE + rows_n, 2)
    for f in range(2):
        rows = halo_rows(links, me, on_in, off_in, f)
        for side, link, over, under in ((0, 2, 4, 6), (1, 3, 5, 7)):
            outer, mine = (0, 2) if side == 0 else (6, 4)

            def sent(entry):
                tile = links[0, entry]
                piece = received[jnp.maximum(tile, 0), f].astype(jnp.float32)
                return jnp.where(tile >= 0, piece, 0.0)

            beside, corner_over, corner_under = sent(link), sent(over), sent(under)
            for c in range(2):
                store[f, mine + c, pl.ds(BASE, rows_n)] = own[side, f, c].astype(jnp.float32)
                store[f, outer + c, pl.ds(BASE, rows_n)] = beside[c]
                store[f, outer + c, low] = corner_over[c, rows_n - 2 : rows_n]
                store[f, outer + c, high] = corner_under[c, 0:2]
            at = 0 if side == 0 else cols_n - 16
            first = 0 if side == 0 else 14
            for where, halo in ((BASE - 2, rows[0]), (BASE + rows_n, rows[1])):
                edge = halo[:, at : at + 16].astype(jnp.float32)
                for r in range(2):
                    for c in range(2):
                        store[f, mine + c, pl.ds(where + r, 1)] = edge[r, first + c : first + c + 1]
        target = (lhs_s, lhs_c)[f]
        for column, base in enumerate((0, 1, 4, 5)):
            for a in range(3):
                for b in range(3):
                    lanes = pl.ds((3 * a + b) * chans, chans)
                    column_in = store.at[f, base + b]
                    target[pl.ds(column * span, rows_n), lanes] = column_in[
                        pl.ds(BASE - 1 + a, rows_n)
                    ].astype(jnp.bfloat16)
                    ends = [column_in[pl.ds(BASE - 2 + a, 8)], column_in[pl.ds(BASE + rows_n - 1 + a, 8)]]
                    target[pl.ds(column * span + rows_n, 16), lanes] = jnp.concatenate(ends, 0).astype(
                        jnp.bfloat16
                    )
    hidden, slope = gelu_pair(dot(lhs_s[...], w_pre[...]))
    grads = dot(lhs_c[...], w_back[...]) * slope
    valid = ((2, 4, 6), (None, 0, 1), (None, 0, 1), (3, 5, 7))
    for column in range(4):
        spans = ((0, rows_n), (rows_n, 8), (rows_n + 8, 8))
        for entry, (start, count) in zip(valid[column], spans):
            start += column * span
            piece = grads[start : start + count]
            if entry is not None:
                piece = jnp.where(links[0, entry] >= 0, piece, 0.0)
            edge_grad[pl.ds(start, count)] = piece.astype(jnp.bfloat16).astype(jnp.float32)

    def inner(values):
        return jnp.concatenate([values[span : span + rows_n], values[2 * span : 2 * span + rows_n]], 0)

    def inner_of(ref):
        return jnp.concatenate([ref[pl.ds(span, rows_n)], ref[pl.ds(2 * span, rows_n)]], 0)

    def over_cells(a, b):
        return lax.dot_general(a, b, (((0,), (0,)), ((), ())), preferred_element_type=jnp.float32)

    first_p = over_cells(inner_of(lhs_s), inner(grads).astype(jnp.bfloat16))
    second_p = over_cells(inner(hidden).astype(jnp.bfloat16), inner_of(lhs_c))
    even = lax.rem(me, 2) == 0
    for tap in range(9):
        part = slice(tap * chans, (tap + 1) * chans)
        first = first_acc[tap] + diagonal(first_p[part], mask, width)
        turned = slice((8 - tap) * chans, (9 - tap) * chans)
        second = second_acc[tap] + diagonal(second_p[:, turned], mask, width)
        keep[tap] = jnp.where(even, first, second)
        pass_on[tap] = jnp.where(even, second, first)


def edge_part(links, me, own, received, on_in, off_in, first_k, second_k, first_acc, second_acc):
    rows_n, chans = own.shape[3:]
    cells = 4 * (rows_n + 16)
    return pl.pallas_call(
        edge_kernel,
        in_specs=[SMEM, SMEM] + [VMEM] * 8,
        out_specs=[VMEM] * 3,
        out_shape=[
            shape_of(first_acc.shape, jnp.float32),
            shape_of(first_acc.shape, jnp.float32),
            shape_of((cells, chans), jnp.float32),
        ],
        scratch_shapes=[
            pltpu.VMEM((2, 8, rows_n + 32, chans), jnp.float32),
            pltpu.VMEM((cells, 9 * chans), jnp.bfloat16),
            pltpu.VMEM((cells, 9 * chans), jnp.bfloat16),
            pltpu.VMEM((9 * chans, chans), jnp.bfloat16),
            pltpu.VMEM((9 * chans, chans), jnp.bfloat16),
        ],
        compiler_params=pltpu.CompilerParams(vmem_limit_bytes=8 * MIB),
        cost_estimate=pl.CostEstimate(flops=200 << 20, bytes_accessed=3 << 20, transcendentals=1 << 15),
        name="edge",
    )(links, me, own, received, on_in, off_in, first_k, second_k, first_acc, second_acc)


def state_kernel(grad, edge_grad, first_k, cot, out, g3, w_state):
    rows_n, cols_n, chans = cot.shape
    fill_paired(w_state, first_k, same_level(first_k.shape[2], chans), True)
    span = rows_n + 16
    x = lax.broadcasted_iota(jnp.int32, (cols_n, chans), 0)
    at_left, at_right = x == 0, x == cols_n - 1

    for row in range(rows_n + 2):
        at = rows_n if row == 0 else rows_n + 8 if row == rows_n + 1 else row - 1
        ends = [edge_grad[number * span + at : number * span + at + 1] for number in range(4)]
        values = grad[row // 2, row % 2].astype(jnp.float32)
        values = jnp.where(at_left, ends[1], jnp.where(at_right, ends[2], values))
        left = jnp.where(at_left, ends[0], pltpu.roll(values, 1, 0))
        right = jnp.where(at_right, ends[3], pltpu.roll(values, cols_n - 1, 0))
        for part, piece in enumerate((left, values, right)):
            g3[row // 2, row % 2, :, part * chans : (part + 1) * chans] = piece.astype(g3.dtype)
    for pair, count in spans_of(rows_n // 2, 4):
        back = dot(windows(g3, pair, count), w_state[...])
        for row in range(2):
            piece = back[:, row * chans : (row + 1) * chans].reshape(count, cols_n, chans)
            for k in range(count):
                y = 2 * (pair + k) + row
                out[y] = (cot[y].astype(jnp.float32) + piece[k]).astype(out.dtype)


def state_part(grad, edge_grad, first_k, cot):
    rows_n, cols_n, chans = cot.shape
    return pl.pallas_call(
        state_kernel,
        in_specs=[VMEM] * 4,
        out_specs=VMEM,
        out_shape=shape_of(cot.shape, jnp.bfloat16),
        scratch_shapes=[
            pltpu.VMEM((rows_n // 2 + 1, 2, cols_n, 3 * chans), jnp.bfloat16),
            pltpu.VMEM((12 * chans, 2 * chans), jnp.bfloat16),
        ],
        compiler_params=pltpu.CompilerParams(vmem_limit_bytes=12 * MIB),
        cost_estimate=pl.CostEstimate(flops=1200 << 20, bytes_accessed=3 << 20, transcendentals=0),
        name="state",
    )(grad, edge_grad, first_k, cot)


def exchanged(value, tiles, pairs):
    both = [(a, b) for a, b in pairs if a < tiles and b < tiles]
    return lax.ppermute(value, "tiles", both + [(b, a) for a, b in both])


def summed(keep, pass_on, me, tiles, scale, edges, state_of):
    even = lax.rem(me, 2) == 0
    if tiles & (tiles - 1):
        first, second = jnp.where(even, keep, pass_on), jnp.where(even, pass_on, keep)
        first, second = lax.psum((first, second), "tiles")
        return first * scale, second * scale, state_of(edges)
    on_chip = [(t, t + 1) for t in range(0, tiles, 2)]
    total = keep + exchanged(pass_on, tiles, on_chip)
    distance = 2
    while distance < tiles:
        last = 2 * distance >= tiles
        if last:
            total, edges = lax.optimization_barrier((total, edges))
        other = exchanged(total, tiles, [(t, t + distance) for t in range(tiles) if not t & distance])
        if last:
            other, state_grad = lax.optimization_barrier((other, state_of(edges)))
        total = total + other
        distance *= 2
    total = total * scale
    other = exchanged(total, tiles, on_chip)
    return jnp.where(even, total, other), jnp.where(even, other, total), state_grad


def local(ocean_state, cotangent, first_kernel, second_kernel, neighbours):
    state, cot = ocean_state[0], cotangent[0]
    rows_n, cols_n, chans = state.shape
    tiles = lax.axis_size("tiles")
    index = lax.axis_index("tiles")
    me = jnp.reshape(index, (1,)).astype(jnp.int32)
    on_out, off_out = pack_rows(neighbours, me, state, cot)
    on_in = exchanged(on_out, tiles, [(t, t + 1) for t in range(0, tiles, 2)])
    off_in = exchanged(off_out, tiles, [(t, t + 1) for t in range(1, tiles, 2)])
    send, own = pack_columns(tiles, me, off_out, state, cot)
    received = lax.all_to_all(send, "tiles", 0, 0)
    grad, first_acc, second_acc = main_part(
        neighbours, me, state, cot, on_in, off_in, first_kernel, second_kernel
    )
    keep, pass_on, edge_grad = edge_part(
        neighbours, me, own, received, on_in, off_in, first_kernel, second_kernel, first_acc, second_acc
    )
    scale = 1.0 / math.sqrt(tiles * rows_n * cols_n)

    def state_of(edges):
        return state_part(grad, edges, first_kernel, cot)

    first, second, state_grad = summed(keep, pass_on, index, tiles, scale, edge_grad, state_of)
    shape = first_kernel.shape
    return state_grad[None], first.reshape(shape), second.reshape(shape)


def solution(mesh):
    placed = (
        P(("groups", "tiles"), None, None, None),
        P(("groups", "tiles"), None, None, None),
        P(),
        P(),
        P("tiles", None),
    )
    return jax.shard_map(
        local,
        mesh=mesh,
        in_specs=placed,
        out_specs=(
            P(("groups", "tiles"), None, None, None),
            P("groups", None, None, None),
            P("groups", None, None, None),
        ),
        check_vma=False,
    )
```

```python
import functools
import math

import jax
import jax.numpy as jnp
from jax import lax
from jax.experimental import pallas as pl
from jax.experimental.pallas import tpu as pltpu
from jax.sharding import PartitionSpec as P

CUBE = 0.044715
ROOT = math.sqrt(2.0 / math.pi)
MIB = 1 << 20
SMEM = pl.BlockSpec(memory_space=pltpu.SMEM)
VMEM = pl.BlockSpec(memory_space=pltpu.VMEM)


def shape_of(dims, dtype):
    return jax.ShapeDtypeStruct(dims, dtype)


def partners(me):
    odd = lax.rem(me, 2)
    return me + 1 - 2 * odd, me - 1 + 2 * odd


def gelu_pair(v):
    square = v * v
    t = jnp.tanh(ROOT * v * (1.0 + CUBE * square))
    half = 0.5 * (1.0 + t)
    slope = half + (0.5 * ROOT) * v * (1.0 - t * t) * (1.0 + (3.0 * CUBE) * square)
    return v * half, slope


def pack_kernel(links, me_ref, *refs):
    blocks, (own, on_out, off_out) = refs[:8], refs[8:]
    me = me_ref[0]
    for f in range(2):
        for side, first in ((0, 0), (1, 14)):
            values = blocks[4 * f + 2 + side][...].astype(jnp.float32)
            for c in range(2):
                own[side, f, c] = values[:, first + c, :].astype(jnp.bfloat16)
    odd = lax.rem(me, 2) == 1
    other = jnp.where(odd, own[:, 0], own[:, 1])
    on_out[4] = other.reshape(on_out.shape[1:])
    for target, out in zip(partners(me), (on_out, off_out)):
        for f in range(2):
            top, bottom = blocks[4 * f][...], blocks[4 * f + 1][...]
            rows = jnp.where(links[0, 1] == target, bottom, jnp.zeros_like(bottom))
            out[2 * f : 2 * f + 2] = jnp.where(links[0, 0] == target, top, rows)


def pack(links, me, state, cot):
    rows_n, cols_n, chans = state.shape
    specs = [
        pl.BlockSpec((2, cols_n, chans), lambda i: (0, 0, 0)),
        pl.BlockSpec((2, cols_n, chans), lambda i: (rows_n // 2 - 1, 0, 0)),
        pl.BlockSpec((rows_n, 16, chans), lambda i: (0, 0, 0)),
        pl.BlockSpec((rows_n, 16, chans), lambda i: (0, cols_n // 16 - 1, 0)),
    ]
    return pl.pallas_call(
        pack_kernel,
        grid=(1,),
        in_specs=[SMEM, SMEM] + specs * 2,
        out_specs=[VMEM] * 3,
        out_shape=[
            shape_of((2, 2, 2, rows_n, chans), jnp.bfloat16),
            shape_of((5, 4 * rows_n, chans), jnp.bfloat16),
            shape_of((4, cols_n, chans), jnp.bfloat16),
        ],
        compiler_params=pltpu.CompilerParams(vmem_limit_bytes=60 * MIB),
        name="pack",
    )(links, me, *([state] * 4), *([cot] * 4))


def slot_kernel(chips, me_ref, own, on_in, send):
    me = me_ref[0]
    chip, odd = me // 2, lax.rem(me, 2) == 1
    mine = jnp.where(odd, own[:, 1], own[:, 0])
    other = on_in[4].reshape(mine.shape)
    low, high = jnp.where(odd, other, mine), jnp.where(odd, mine, other)

    def fill(j, carry):
        send[j, 0] = jnp.where(j >= chip, low[1], low[0])
        send[j, 1] = jnp.where(j > chip, high[1], high[0])
        return carry

    lax.fori_loop(0, chips, fill, 0)


def slots(chips, me, own, on_in):
    return pl.pallas_call(
        functools.partial(slot_kernel, chips),
        in_specs=[SMEM] + [VMEM] * 2,
        out_specs=VMEM,
        out_shape=shape_of((chips, 2) + own.shape[2:], jnp.bfloat16),
        compiler_params=pltpu.CompilerParams(vmem_limit_bytes=24 * MIB),
        name="slots",
    )(me, own, on_in)


def halo_rows(links, me, on_in, off_in, f):
    found = []
    for link in (0, 1):
        rows = jnp.zeros((2,) + off_in.shape[1:], off_in.dtype)
        for source, packet in zip(partners(me), (on_in, off_in)):
            rows = jnp.where(links[0, link] == source, packet[2 * f : 2 * f + 2], rows)
        found.append(rows)
    return found


def same_level(width, chans):
    down = lax.broadcasted_iota(jnp.int32, (chans, chans), 0) // width
    across = lax.broadcasted_iota(jnp.int32, (chans, chans), 1) // width
    return down == across


def diagonal(product, mask, width):
    kept = jnp.where(mask, product, 0.0)
    return sum(kept[at : at + width] for at in range(0, product.shape[0], width))


def thirds(ref, row, values):
    count, cols_n, chans = values.shape
    flat = values.reshape(count * cols_n, chans).astype(jnp.float32)
    left = pltpu.roll(flat, 1, 0).astype(ref.dtype)
    right = pltpu.roll(flat, count * cols_n - 1, 0).astype(ref.dtype)
    for part, piece in enumerate((left, values, right)):
        lanes = slice(part * chans, (part + 1) * chans)
        ref[pl.ds(row // 2, count // 2), :, :, lanes] = piece.reshape(count // 2, 2, cols_n, chans)


def windows(ref, pair, count):
    parts = []
    for row in range(4):
        rows = ref[pl.ds(pair + row // 2, count), row % 2]
        parts.append(rows.reshape(count * rows.shape[1], rows.shape[2]))
    return jnp.concatenate(parts, 1)


def dot(a, b):
    return jnp.dot(a, b, preferred_element_type=jnp.float32)


def spans_of(total, most):
    count = pl.cdiv(total, most)
    bounds = [total * i // count for i in range(count + 1)]
    return [(lo, hi - lo) for lo, hi in zip(bounds, bounds[1:])]


def level_blocks(kernel, tap, mask):
    block = kernel[tap // 3, tap % 3].astype(jnp.float32)
    return jnp.where(mask, jnp.concatenate([block] * (mask.shape[0] // block.shape[0]), 0), 0.0)


def fill_paired(ref, kernel, mask, turned):
    chans = mask.shape[0]
    none = jnp.zeros((3 * chans, chans), ref.dtype)
    ref[9 * chans : 12 * chans, 0:chans] = none
    ref[0 : 3 * chans, chans : 2 * chans] = none
    for tap in range(9):
        dense = level_blocks(kernel, tap, mask)
        if turned:
            paired(ref, 8 - tap, dense.T.astype(ref.dtype))
        else:
            paired(ref, tap, dense.astype(ref.dtype))


def paired(ref, tap, dense):
    chans = dense.shape[0]
    for row in range(2):
        ref[pl.ds((tap + 3 * row) * chans, chans), row * chans : (row + 1) * chans] = dense


def main_kernel(
    links, me_ref, state, cot, on_in, off_in, first_k, second_k,
    grad, first_acc, second_acc,
    w_pre, w_back, s3, c3, acc1, acc2, grad_v, sem,
):
    me = me_ref[0]
    rows_n, cols_n, chans = state.shape
    width = first_k.shape[2]
    mask = same_level(width, chans)
    fill_paired(w_pre, first_k, mask, False)
    fill_paired(w_back, second_k, mask, True)
    for f, (field, store) in enumerate(((state, s3), (cot, c3))):
        above, below = halo_rows(links, me, on_in, off_in, f)
        thirds(store, 0, above)
        thirds(store, rows_n + 2, below)
        for row, count in spans_of(rows_n // 2, 4):
            thirds(store, 2 * row + 2, field[pl.ds(2 * row, 2 * count)])

    acc1[...] = jnp.zeros_like(acc1)
    acc2[...] = jnp.zeros_like(acc2)
    pairs_n = rows_n // 2 + 1
    copies = []
    for k, (pair, count) in enumerate(spans_of(pairs_n, PAIRS)):
        near_state, near_cot = windows(s3, pair, count), windows(c3, pair, count)
        hidden, slope = gelu_pair(dot(near_state, w_pre[...]))
        grads = dot(near_cot, w_back[...]) * slope
        cell = lax.broadcasted_iota(jnp.int32, grads.shape, 0)
        lane = lax.broadcasted_iota(jnp.int32, grads.shape, 1)
        x = lax.rem(cell, cols_n)
        inner = (x > 0) & (x < cols_n - 1)
        if pair == 0:
            outside = (cell < cols_n) & (lane < chans)
            inner = inner & ~outside
            grads = jnp.where(outside & (links[0, 0] < 0), 0.0, grads)
        if pair + count == pairs_n:
            outside = (cell >= (count - 1) * cols_n) & (lane >= chans)
            inner = inner & ~outside
            grads = jnp.where(outside & (links[0, 1] < 0), 0.0, grads)
        for row in range(2):
            piece = grads[:, row * chans : (row + 1) * chans].astype(jnp.bfloat16)
            grad_v[pl.ds(pair, count), row] = piece.reshape(count, cols_n, chans)
        part = pl.ds(pair, count)
        copies.append(pltpu.make_async_copy(grad_v.at[part], grad.at[part], sem.at[k]))
        copies[-1].start()
        grads = jnp.where(inner, grads, 0.0).astype(jnp.bfloat16)
        hidden = jnp.where(inner, hidden, 0.0).astype(jnp.bfloat16)
        acc1[...] += dot(grads.T, near_state)
        acc2[...] += dot(hidden.T, near_cot)
    for tap in range(9):
        one, two = (slice((tap + 3 * r) * chans, (tap + 3 * r + 1) * chans) for r in range(2))
        first = acc1[0:chans, one] + acc1[chans : 2 * chans, two]
        second = acc2[0:chans, one] + acc2[chans : 2 * chans, two]
        first_acc[tap] = diagonal(first.T, mask, width)
        second_acc[8 - tap] = diagonal(second, mask, width)
    for copy in copies:
        copy.wait()


PAIRS = 9


def main_part(links, me, state, cot, on_in, off_in, first_k, second_k):
    rows_n, cols_n, chans = state.shape
    width = first_k.shape[2]
    flops = 2 * rows_n * cols_n * 9 * chans * chans * 4
    return pl.pallas_call(
        main_kernel,
        in_specs=[SMEM, SMEM] + [VMEM] * 6,
        out_specs=[pl.BlockSpec(memory_space=pltpu.HBM), VMEM, VMEM],
        out_shape=[
            pltpu.HBM((rows_n // 2 + 1, 2, cols_n, chans), jnp.bfloat16),
            shape_of((9, width, chans), jnp.float32),
            shape_of((9, width, chans), jnp.float32),
        ],
        scratch_shapes=[
            pltpu.VMEM((12 * chans, 2 * chans), jnp.bfloat16),
            pltpu.VMEM((12 * chans, 2 * chans), jnp.bfloat16),
            pltpu.VMEM((rows_n // 2 + 2, 2, cols_n, 3 * chans), jnp.bfloat16),
            pltpu.VMEM((rows_n // 2 + 2, 2, cols_n, 3 * chans), jnp.bfloat16),
            pltpu.VMEM((2 * chans, 12 * chans), jnp.float32),
            pltpu.VMEM((2 * chans, 12 * chans), jnp.float32),
            pltpu.VMEM((rows_n // 2 + 1, 2, cols_n, chans), jnp.bfloat16),
            pltpu.SemaphoreType.DMA((len(spans_of(rows_n // 2 + 1, PAIRS)),)),
        ],
        compiler_params=pltpu.CompilerParams(vmem_limit_bytes=26 * MIB),
        cost_estimate=pl.CostEstimate(flops=20 * flops, bytes_accessed=5 << 20, transcendentals=1 << 19),
        name="main",
    )(links, me, state, cot, on_in, off_in, first_k, second_k)


BASE = 16


def edge_kernel(
    links, me_ref, own, received, other_in, on_in, off_in, first_k, second_k, first_acc, second_acc,
    keep, pass_on, edge_grad, store, lhs_s, lhs_c, w_pre, w_back,
):
    me = me_ref[0]
    rows_n, chans = own.shape[3], own.shape[4]
    cols_n = off_in.shape[1]
    odd = lax.rem(me, 2) == 1
    width = first_acc.shape[1]
    span = rows_n + 16
    mask = same_level(width, chans)
    for tap in range(9):
        at = slice(tap * chans, (tap + 1) * chans)
        w_pre[at] = level_blocks(first_k, tap, mask).astype(w_pre.dtype)
        w_back[at] = level_blocks(second_k, 8 - tap, mask).T.astype(w_back.dtype)
    store[...] = jnp.zeros_like(store)
    low, high = pl.ds(BASE - 2, 2), pl.ds(BASE + rows_n, 2)
    for f in range(2):
        rows = halo_rows(links, me, on_in, off_in, f)
        for side, link, over, under in ((0, 2, 4, 6), (1, 3, 5, 7)):
            outer, mine = (0, 2) if side == 0 else (6, 4)

            def sent(entry):
                tile = links[0, entry]
                at = jnp.maximum(tile, 0)
                pieces = (received[at], other_in[at])[:: 1 - 2 * f]
                piece = jnp.where(odd, pieces[1], pieces[0]).astype(jnp.float32)
                return jnp.where(tile >= 0, piece, 0.0)

            beside, corner_over, corner_under = sent(link), sent(over), sent(under)
            for c in range(2):
                store[f, mine + c, pl.ds(BASE, rows_n)] = own[side, f, c].astype(jnp.float32)
                store[f, outer + c, pl.ds(BASE, rows_n)] = beside[c]
                store[f, outer + c, low] = corner_over[c, rows_n - 2 : rows_n]
                store[f, outer + c, high] = corner_under[c, 0:2]
            at = 0 if side == 0 else cols_n - 16
            first = 0 if side == 0 else 14
            for where, halo in ((BASE - 2, rows[0]), (BASE + rows_n, rows[1])):
                edge = halo[:, at : at + 16].astype(jnp.float32)
                for r in range(2):
                    for c in range(2):
                        store[f, mine + c, pl.ds(where + r, 1)] = edge[r, first + c : first + c + 1]
        target = (lhs_s, lhs_c)[f]
        for column, base in enumerate((0, 1, 4, 5)):
            for a in range(3):
                for b in range(3):
                    lanes = pl.ds((3 * a + b) * chans, chans)
                    column_in = store.at[f, base + b]
                    target[pl.ds(column * span, rows_n), lanes] = column_in[
                        pl.ds(BASE - 1 + a, rows_n)
                    ].astype(jnp.bfloat16)
                    ends = [column_in[pl.ds(BASE - 2 + a, 8)], column_in[pl.ds(BASE + rows_n - 1 + a, 8)]]
                    target[pl.ds(column * span + rows_n, 16), lanes] = jnp.concatenate(ends, 0).astype(
                        jnp.bfloat16
                    )
    hidden, slope = gelu_pair(dot(lhs_s[...], w_pre[...]))
    grads = dot(lhs_c[...], w_back[...]) * slope
    valid = ((2, 4, 6), (None, 0, 1), (None, 0, 1), (3, 5, 7))
    for column in range(4):
        spans = ((0, rows_n), (rows_n, 8), (rows_n + 8, 8))
        for entry, (start, count) in zip(valid[column], spans):
            start += column * span
            piece = grads[start : start + count]
            if entry is not None:
                piece = jnp.where(links[0, entry] >= 0, piece, 0.0)
            edge_grad[pl.ds(start, count)] = piece.astype(jnp.bfloat16).astype(jnp.float32)

    def inner(values):
        return jnp.concatenate([values[span : span + rows_n], values[2 * span : 2 * span + rows_n]], 0)

    def inner_of(ref):
        return jnp.concatenate([ref[pl.ds(span, rows_n)], ref[pl.ds(2 * span, rows_n)]], 0)

    def over_cells(a, b):
        return lax.dot_general(a, b, (((0,), (0,)), ((), ())), preferred_element_type=jnp.float32)

    first_p = over_cells(inner_of(lhs_s), inner(grads).astype(jnp.bfloat16))
    second_p = over_cells(inner(hidden).astype(jnp.bfloat16), inner_of(lhs_c))
    even = lax.rem(me, 2) == 0
    for tap in range(9):
        part = slice(tap * chans, (tap + 1) * chans)
        first = first_acc[tap] + diagonal(first_p[part], mask, width)
        turned = slice((8 - tap) * chans, (9 - tap) * chans)
        second = second_acc[tap] + diagonal(second_p[:, turned], mask, width)
        keep[tap] = jnp.where(even, first, second)
        pass_on[tap] = jnp.where(even, second, first)


def edge_part(links, me, own, received, other_in, on_in, off_in, first_k, second_k, first_acc, second_acc):
    rows_n, chans = own.shape[3:]
    cells = 4 * (rows_n + 16)
    return pl.pallas_call(
        edge_kernel,
        in_specs=[SMEM, SMEM] + [VMEM] * 9,
        out_specs=[VMEM] * 3,
        out_shape=[
            shape_of(first_acc.shape, jnp.float32),
            shape_of(first_acc.shape, jnp.float32),
            shape_of((cells, chans), jnp.float32),
        ],
        scratch_shapes=[
            pltpu.VMEM((2, 8, rows_n + 32, chans), jnp.float32),
            pltpu.VMEM((cells, 9 * chans), jnp.bfloat16),
            pltpu.VMEM((cells, 9 * chans), jnp.bfloat16),
            pltpu.VMEM((9 * chans, chans), jnp.bfloat16),
            pltpu.VMEM((9 * chans, chans), jnp.bfloat16),
        ],
        compiler_params=pltpu.CompilerParams(vmem_limit_bytes=8 * MIB),
        cost_estimate=pl.CostEstimate(flops=200 << 20, bytes_accessed=3 << 20, transcendentals=1 << 15),
        name="edge",
    )(links, me, own, received, other_in, on_in, off_in, first_k, second_k, first_acc, second_acc)


def state_kernel(grad, edge_grad, first_k, cot, out, g3, w_state):
    rows_n, cols_n, chans = cot.shape
    fill_paired(w_state, first_k, same_level(first_k.shape[2], chans), True)
    span = rows_n + 16
    x = lax.broadcasted_iota(jnp.int32, (cols_n, chans), 0)
    at_left, at_right = x == 0, x == cols_n - 1

    for row in range(rows_n + 2):
        at = rows_n if row == 0 else rows_n + 8 if row == rows_n + 1 else row - 1
        ends = [edge_grad[number * span + at : number * span + at + 1] for number in range(4)]
        values = grad[row // 2, row % 2].astype(jnp.float32)
        values = jnp.where(at_left, ends[1], jnp.where(at_right, ends[2], values))
        left = jnp.where(at_left, ends[0], pltpu.roll(values, 1, 0))
        right = jnp.where(at_right, ends[3], pltpu.roll(values, cols_n - 1, 0))
        for part, piece in enumerate((left, values, right)):
            g3[row // 2, row % 2, :, part * chans : (part + 1) * chans] = piece.astype(g3.dtype)
    for pair, count in spans_of(rows_n // 2, 4):
        back = dot(windows(g3, pair, count), w_state[...])
        for row in range(2):
            piece = back[:, row * chans : (row + 1) * chans].reshape(count, cols_n, chans)
            for k in range(count):
                y = 2 * (pair + k) + row
                out[y] = (cot[y].astype(jnp.float32) + piece[k]).astype(out.dtype)


def state_part(grad, edge_grad, first_k, cot):
    rows_n, cols_n, chans = cot.shape
    return pl.pallas_call(
        state_kernel,
        in_specs=[VMEM] * 4,
        out_specs=VMEM,
        out_shape=shape_of(cot.shape, jnp.bfloat16),
        scratch_shapes=[
            pltpu.VMEM((rows_n // 2 + 1, 2, cols_n, 3 * chans), jnp.bfloat16),
            pltpu.VMEM((12 * chans, 2 * chans), jnp.bfloat16),
        ],
        compiler_params=pltpu.CompilerParams(vmem_limit_bytes=12 * MIB),
        cost_estimate=pl.CostEstimate(flops=1200 << 20, bytes_accessed=3 << 20, transcendentals=0),
        name="state",
    )(grad, edge_grad, first_k, cot)


def exchanged(value, tiles, pairs):
    both = [(a, b) for a, b in pairs if a < tiles and b < tiles]
    return lax.ppermute(value, "tiles", both + [(b, a) for a, b in both])


def summed(keep, pass_on, me, tiles, scale, edges, state_of):
    even = lax.rem(me, 2) == 0
    if tiles & (tiles - 1):
        first, second = jnp.where(even, keep, pass_on), jnp.where(even, pass_on, keep)
        first, second = lax.psum((first, second), "tiles")
        return first * scale, second * scale, state_of(edges)
    on_chip = [(t, t + 1) for t in range(0, tiles, 2)]
    total = keep + exchanged(pass_on, tiles, on_chip)
    distance = 2
    while distance < tiles:
        last = 2 * distance >= tiles
        if last:
            total, edges = lax.optimization_barrier((total, edges))
        other = exchanged(total, tiles, [(t, t + distance) for t in range(tiles) if not t & distance])
        if last:
            other, state_grad = lax.optimization_barrier((other, state_of(edges)))
        total = total + other
        distance *= 2
    total = total * scale
    other = exchanged(total, tiles, on_chip)
    return jnp.where(even, total, other), jnp.where(even, other, total), state_grad


def local(ocean_state, cotangent, first_kernel, second_kernel, neighbours):
    state, cot = ocean_state[0], cotangent[0]
    rows_n, cols_n, chans = state.shape
    tiles = lax.axis_size("tiles")
    index = lax.axis_index("tiles")
    me = jnp.reshape(index, (1,)).astype(jnp.int32)
    own, on_out, off_out = pack(neighbours, me, state, cot)
    on_chip = [(t, t + 1) for t in range(0, tiles, 2)]
    on_in = exchanged(on_out, tiles, on_chip)
    off_in = exchanged(off_out, tiles, [(t, t + 1) for t in range(1, tiles, 2)])
    cores = [list(range(core, tiles, 2)) for core in range(2)]
    sent = slots(tiles // 2, me, own, on_in)
    received = lax.all_to_all(sent, "tiles", 0, 0, axis_index_groups=cores)
    received = received.reshape((tiles,) + received.shape[2:])
    grad, first_acc, second_acc = main_part(
        neighbours, me, state, cot, on_in, off_in, first_kernel, second_kernel
    )
    received, first_acc = lax.optimization_barrier((received, first_acc))
    other_in = exchanged(received, tiles, on_chip)
    keep, pass_on, edge_grad = edge_part(
        neighbours, me, own, received, other_in, on_in, off_in, first_kernel, second_kernel, first_acc, second_acc
    )
    scale = 1.0 / math.sqrt(tiles * rows_n * cols_n)

    def state_of(edges):
        return state_part(grad, edges, first_kernel, cot)

    first, second, state_grad = summed(keep, pass_on, index, tiles, scale, edge_grad, state_of)
    shape = first_kernel.shape
    return state_grad[None], first.reshape(shape), second.reshape(shape)


def solution(mesh):
    placed = (
        P(("groups", "tiles"), None, None, None),
        P(("groups", "tiles"), None, None, None),
        P(),
        P(),
        P("tiles", None),
    )
    return jax.shard_map(
        local,
        mesh=mesh,
        in_specs=placed,
        out_specs=(
            P(("groups", "tiles"), None, None, None),
            P("groups", None, None, None),
            P("groups", None, None, None),
        ),
        check_vma=False,
    )
```

```python
import functools
import math

import jax
import jax.numpy as jnp
from jax import lax
from jax.experimental import pallas as pl
from jax.experimental.pallas import tpu as pltpu
from jax.sharding import PartitionSpec as P

CUBE = 0.044715
ROOT = math.sqrt(2.0 / math.pi)
MIB = 1 << 20
PACK = 8
SMEM = pl.BlockSpec(memory_space=pltpu.SMEM)
VMEM = pl.BlockSpec(memory_space=pltpu.VMEM)


def shape_of(dims, dtype):
    return jax.ShapeDtypeStruct(dims, dtype)


def partners(me):
    odd = lax.rem(me, 2)
    return me + 1 - 2 * odd, me - 1 + 2 * odd


def gelu_pair(v):
    square = v * v
    t = jnp.tanh(ROOT * v * (1.0 + CUBE * square))
    half = 0.5 * (1.0 + t)
    slope = half + (0.5 * ROOT) * v * (1.0 - t * t) * (1.0 + (3.0 * CUBE) * square)
    return v * half, slope


def pack_kernel(links_in, me_ref, state, cot, own, on_out, off_out, rows, columns, links, sem, links_sem):
    rows_n, cols_n, chans = state.shape
    me = me_ref[0]
    copies = [pltpu.make_async_copy(links_in, links, links_sem)]
    for f, field in enumerate((state, cot)):
        for side in range(2):
            beside = field.at[:, pl.ds(side * (cols_n - 16), 16)]
            copies.append(pltpu.make_async_copy(beside, columns.at[f, side], sem.at[f, side]))
            outer = field.at[pl.ds(side * (rows_n - 2), 2)]
            copies.append(pltpu.make_async_copy(outer, rows.at[f, side], sem.at[f, 2 + side]))
    for copy in copies:
        copy.start()
    for copy in copies:
        copy.wait()
    for f in range(2):
        for side, first in ((0, 0), (1, 14)):
            values = columns[f, side].astype(jnp.float32)
            for c in range(2):
                own[side, f, c] = values[:, first + c, :].astype(jnp.bfloat16)
    odd = lax.rem(me, 2) == 1
    other = jnp.where(odd, own[:, 0], own[:, 1])
    on_out[4] = other.reshape(on_out.shape[1:])
    for target, out in zip(partners(me), (on_out, off_out)):
        for f in range(2):
            top, bottom = rows[f, 0], rows[f, 1]
            sent = jnp.where(links[0, 1] == target, bottom, jnp.zeros_like(bottom))
            out[2 * f : 2 * f + 2] = jnp.where(links[0, 0] == target, top, sent)


def pack(links, me, state, cot):
    rows_n, cols_n, chans = state.shape
    far = pl.BlockSpec(memory_space=pltpu.HBM)
    placed = functools.partial(pltpu.with_memory_space_constraint, memory_space=pltpu.HBM)
    return pl.pallas_call(
        pack_kernel,
        in_specs=[far, SMEM, far, far],
        out_specs=[VMEM] * 3,
        out_shape=[
            shape_of((2, 2, 2, rows_n, chans), jnp.bfloat16),
            shape_of((5, 4 * rows_n, chans), jnp.bfloat16),
            shape_of((4, cols_n, chans), jnp.bfloat16),
        ],
        scratch_shapes=[
            pltpu.VMEM((2, 2, 2, cols_n, chans), jnp.bfloat16),
            pltpu.VMEM((2, 2, rows_n, 16, chans), jnp.bfloat16),
            pltpu.SMEM(links.shape, links.dtype),
            pltpu.SemaphoreType.DMA((2, 4)),
            pltpu.SemaphoreType.DMA,
        ],
        compiler_params=pltpu.CompilerParams(vmem_limit_bytes=PACK * MIB),
        name="pack",
    )(placed(links), me, placed(state), placed(cot))


def slot_kernel(chips, me_ref, own, on_in, send):
    me = me_ref[0]
    chip, odd = me // 2, lax.rem(me, 2) == 1
    mine = jnp.where(odd, own[:, 1], own[:, 0])
    other = on_in[4].reshape(mine.shape)
    low, high = jnp.where(odd, other, mine), jnp.where(odd, mine, other)

    def fill(j, carry):
        send[j, 0] = jnp.where(j >= chip, low[1], low[0])
        send[j, 1] = jnp.where(j > chip, high[1], high[0])
        return carry

    lax.fori_loop(0, chips, fill, 0)


def slots(chips, me, own, on_in):
    return pl.pallas_call(
        functools.partial(slot_kernel, chips),
        in_specs=[SMEM] + [VMEM] * 2,
        out_specs=VMEM,
        out_shape=shape_of((chips, 2) + own.shape[2:], jnp.bfloat16),
        compiler_params=pltpu.CompilerParams(vmem_limit_bytes=24 * MIB),
        name="slots",
    )(me, own, on_in)


def halo_rows(links, me, on_in, off_in, f):
    found = []
    for link in (0, 1):
        rows = jnp.zeros((2,) + off_in.shape[1:], off_in.dtype)
        for source, packet in zip(partners(me), (on_in, off_in)):
            rows = jnp.where(links[0, link] == source, packet[2 * f : 2 * f + 2], rows)
        found.append(rows)
    return found


def same_level(width, chans):
    down = lax.broadcasted_iota(jnp.int32, (chans, chans), 0) // width
    across = lax.broadcasted_iota(jnp.int32, (chans, chans), 1) // width
    return down == across


def diagonal(product, mask, width):
    kept = jnp.where(mask, product, 0.0)
    return sum(kept[at : at + width] for at in range(0, product.shape[0], width))


def thirds(ref, row, values):
    count, cols_n, chans = values.shape
    flat = values.reshape(count * cols_n, chans).astype(jnp.float32)
    left = pltpu.roll(flat, 1, 0).astype(ref.dtype)
    right = pltpu.roll(flat, count * cols_n - 1, 0).astype(ref.dtype)
    for part, piece in enumerate((left, values, right)):
        lanes = slice(part * chans, (part + 1) * chans)
        ref[pl.ds(row // 2, count // 2), :, :, lanes] = piece.reshape(count // 2, 2, cols_n, chans)


def windows(ref, pair, count):
    parts = []
    for row in range(4):
        rows = ref[pl.ds(pair + row // 2, count), row % 2]
        parts.append(rows.reshape(count * rows.shape[1], rows.shape[2]))
    return jnp.concatenate(parts, 1)


def dot(a, b):
    return jnp.dot(a, b, preferred_element_type=jnp.float32)


def spans_of(total, most):
    count = pl.cdiv(total, most)
    bounds = [total * i // count for i in range(count + 1)]
    return [(lo, hi - lo) for lo, hi in zip(bounds, bounds[1:])]


def level_blocks(kernel, tap, mask):
    block = kernel[tap // 3, tap % 3].astype(jnp.float32)
    return jnp.where(mask, jnp.concatenate([block] * (mask.shape[0] // block.shape[0]), 0), 0.0)


def fill_paired(ref, kernel, mask, turned):
    chans = mask.shape[0]
    none = jnp.zeros((3 * chans, chans), ref.dtype)
    ref[9 * chans : 12 * chans, 0:chans] = none
    ref[0 : 3 * chans, chans : 2 * chans] = none
    for tap in range(9):
        dense = level_blocks(kernel, tap, mask)
        if turned:
            paired(ref, 8 - tap, dense.T.astype(ref.dtype))
        else:
            paired(ref, tap, dense.astype(ref.dtype))


def paired(ref, tap, dense):
    chans = dense.shape[0]
    for row in range(2):
        ref[pl.ds((tap + 3 * row) * chans, chans), row * chans : (row + 1) * chans] = dense


def main_kernel(
    links, me_ref, state, cot, on_in, off_in, first_k, second_k,
    grad, first_acc, second_acc,
    w_pre, w_back, s3, c3, acc1, acc2, grad_v, sem,
):
    me = me_ref[0]
    rows_n, cols_n, chans = state.shape
    width = first_k.shape[2]
    mask = same_level(width, chans)
    fill_paired(w_pre, first_k, mask, False)
    fill_paired(w_back, second_k, mask, True)
    for f, (field, store) in enumerate(((state, s3), (cot, c3))):
        above, below = halo_rows(links, me, on_in, off_in, f)
        thirds(store, 0, above)
        thirds(store, rows_n + 2, below)
        for row, count in spans_of(rows_n // 2, 4):
            thirds(store, 2 * row + 2, field[pl.ds(2 * row, 2 * count)])

    acc1[...] = jnp.zeros_like(acc1)
    acc2[...] = jnp.zeros_like(acc2)
    pairs_n = rows_n // 2 + 1
    copies = []
    for k, (pair, count) in enumerate(spans_of(pairs_n, PAIRS)):
        near_state, near_cot = windows(s3, pair, count), windows(c3, pair, count)
        hidden, slope = gelu_pair(dot(near_state, w_pre[...]))
        grads = dot(near_cot, w_back[...]) * slope
        cell = lax.broadcasted_iota(jnp.int32, grads.shape, 0)
        lane = lax.broadcasted_iota(jnp.int32, grads.shape, 1)
        x = lax.rem(cell, cols_n)
        inner = (x > 0) & (x < cols_n - 1)
        if pair == 0:
            outside = (cell < cols_n) & (lane < chans)
            inner = inner & ~outside
            grads = jnp.where(outside & (links[0, 0] < 0), 0.0, grads)
        if pair + count == pairs_n:
            outside = (cell >= (count - 1) * cols_n) & (lane >= chans)
            inner = inner & ~outside
            grads = jnp.where(outside & (links[0, 1] < 0), 0.0, grads)
        for row in range(2):
            piece = grads[:, row * chans : (row + 1) * chans].astype(jnp.bfloat16)
            grad_v[pl.ds(pair, count), row] = piece.reshape(count, cols_n, chans)
        part = pl.ds(pair, count)
        copies.append(pltpu.make_async_copy(grad_v.at[part], grad.at[part], sem.at[k]))
        copies[-1].start()
        grads = jnp.where(inner, grads, 0.0).astype(jnp.bfloat16)
        hidden = jnp.where(inner, hidden, 0.0).astype(jnp.bfloat16)
        acc1[...] += dot(grads.T, near_state)
        acc2[...] += dot(hidden.T, near_cot)
    for tap in range(9):
        one, two = (slice((tap + 3 * r) * chans, (tap + 3 * r + 1) * chans) for r in range(2))
        first = acc1[0:chans, one] + acc1[chans : 2 * chans, two]
        second = acc2[0:chans, one] + acc2[chans : 2 * chans, two]
        first_acc[tap] = diagonal(first.T, mask, width)
        second_acc[8 - tap] = diagonal(second, mask, width)
    for copy in copies:
        copy.wait()


PAIRS = 9


def main_part(links, me, state, cot, on_in, off_in, first_k, second_k):
    rows_n, cols_n, chans = state.shape
    width = first_k.shape[2]
    flops = 2 * rows_n * cols_n * 9 * chans * chans * 4
    return pl.pallas_call(
        main_kernel,
        in_specs=[SMEM, SMEM] + [VMEM] * 6,
        out_specs=[pl.BlockSpec(memory_space=pltpu.HBM), VMEM, VMEM],
        out_shape=[
            pltpu.HBM((rows_n // 2 + 1, 2, cols_n, chans), jnp.bfloat16),
            shape_of((9, width, chans), jnp.float32),
            shape_of((9, width, chans), jnp.float32),
        ],
        scratch_shapes=[
            pltpu.VMEM((12 * chans, 2 * chans), jnp.bfloat16),
            pltpu.VMEM((12 * chans, 2 * chans), jnp.bfloat16),
            pltpu.VMEM((rows_n // 2 + 2, 2, cols_n, 3 * chans), jnp.bfloat16),
            pltpu.VMEM((rows_n // 2 + 2, 2, cols_n, 3 * chans), jnp.bfloat16),
            pltpu.VMEM((2 * chans, 12 * chans), jnp.float32),
            pltpu.VMEM((2 * chans, 12 * chans), jnp.float32),
            pltpu.VMEM((rows_n // 2 + 1, 2, cols_n, chans), jnp.bfloat16),
            pltpu.SemaphoreType.DMA((len(spans_of(rows_n // 2 + 1, PAIRS)),)),
        ],
        compiler_params=pltpu.CompilerParams(vmem_limit_bytes=26 * MIB),
        cost_estimate=pl.CostEstimate(flops=20 * flops, bytes_accessed=5 << 20, transcendentals=1 << 19),
        name="main",
    )(links, me, state, cot, on_in, off_in, first_k, second_k)


BASE = 16


def edge_kernel(
    links, me_ref, own, received, other_in, on_in, off_in, first_k, second_k, first_acc, second_acc,
    keep, pass_on, edge_grad, store, lhs_s, lhs_c, w_pre, w_back,
):
    me = me_ref[0]
    rows_n, chans = own.shape[3], own.shape[4]
    cols_n = off_in.shape[1]
    odd = lax.rem(me, 2) == 1
    width = first_acc.shape[1]
    span = rows_n + 16
    mask = same_level(width, chans)
    for tap in range(9):
        at = slice(tap * chans, (tap + 1) * chans)
        w_pre[at] = level_blocks(first_k, tap, mask).astype(w_pre.dtype)
        w_back[at] = level_blocks(second_k, 8 - tap, mask).T.astype(w_back.dtype)
    store[...] = jnp.zeros_like(store)
    low, high = pl.ds(BASE - 2, 2), pl.ds(BASE + rows_n, 2)
    for f in range(2):
        rows = halo_rows(links, me, on_in, off_in, f)
        for side, link, over, under in ((0, 2, 4, 6), (1, 3, 5, 7)):
            outer, mine = (0, 2) if side == 0 else (6, 4)

            def sent(entry):
                tile = links[0, entry]
                at = jnp.maximum(tile, 0)
                pieces = (received[at], other_in[at])[:: 1 - 2 * f]
                piece = jnp.where(odd, pieces[1], pieces[0]).astype(jnp.float32)
                return jnp.where(tile >= 0, piece, 0.0)

            beside, corner_over, corner_under = sent(link), sent(over), sent(under)
            for c in range(2):
                store[f, mine + c, pl.ds(BASE, rows_n)] = own[side, f, c].astype(jnp.float32)
                store[f, outer + c, pl.ds(BASE, rows_n)] = beside[c]
                store[f, outer + c, low] = corner_over[c, rows_n - 2 : rows_n]
                store[f, outer + c, high] = corner_under[c, 0:2]
            at = 0 if side == 0 else cols_n - 16
            first = 0 if side == 0 else 14
            for where, halo in ((BASE - 2, rows[0]), (BASE + rows_n, rows[1])):
                edge = halo[:, at : at + 16].astype(jnp.float32)
                for r in range(2):
                    for c in range(2):
                        store[f, mine + c, pl.ds(where + r, 1)] = edge[r, first + c : first + c + 1]
        target = (lhs_s, lhs_c)[f]
        for column, base in enumerate((0, 1, 4, 5)):
            for a in range(3):
                for b in range(3):
                    lanes = pl.ds((3 * a + b) * chans, chans)
                    column_in = store.at[f, base + b]
                    target[pl.ds(column * span, rows_n), lanes] = column_in[
                        pl.ds(BASE - 1 + a, rows_n)
                    ].astype(jnp.bfloat16)
                    ends = [column_in[pl.ds(BASE - 2 + a, 8)], column_in[pl.ds(BASE + rows_n - 1 + a, 8)]]
                    target[pl.ds(column * span + rows_n, 16), lanes] = jnp.concatenate(ends, 0).astype(
                        jnp.bfloat16
                    )
    hidden, slope = gelu_pair(dot(lhs_s[...], w_pre[...]))
    grads = dot(lhs_c[...], w_back[...]) * slope
    valid = ((2, 4, 6), (None, 0, 1), (None, 0, 1), (3, 5, 7))
    for column in range(4):
        spans = ((0, rows_n), (rows_n, 8), (rows_n + 8, 8))
        for entry, (start, count) in zip(valid[column], spans):
            start += column * span
            piece = grads[start : start + count]
            if entry is not None:
                piece = jnp.where(links[0, entry] >= 0, piece, 0.0)
            edge_grad[pl.ds(start, count)] = piece.astype(jnp.bfloat16).astype(jnp.float32)

    def inner(values):
        return jnp.concatenate([values[span : span + rows_n], values[2 * span : 2 * span + rows_n]], 0)

    def inner_of(ref):
        return jnp.concatenate([ref[pl.ds(span, rows_n)], ref[pl.ds(2 * span, rows_n)]], 0)

    def over_cells(a, b):
        return lax.dot_general(a, b, (((0,), (0,)), ((), ())), preferred_element_type=jnp.float32)

    first_p = over_cells(inner_of(lhs_s), inner(grads).astype(jnp.bfloat16))
    second_p = over_cells(inner(hidden).astype(jnp.bfloat16), inner_of(lhs_c))
    even = lax.rem(me, 2) == 0
    for tap in range(9):
        part = slice(tap * chans, (tap + 1) * chans)
        first = first_acc[tap] + diagonal(first_p[part], mask, width)
        turned = slice((8 - tap) * chans, (9 - tap) * chans)
        second = second_acc[tap] + diagonal(second_p[:, turned], mask, width)
        keep[tap] = jnp.where(even, first, second)
        pass_on[tap] = jnp.where(even, second, first)
        size = jnp.maximum(jnp.abs(first), jnp.abs(second))
        largest = size if tap == 0 else jnp.maximum(largest, size)
    largest = jnp.max(jnp.max(largest, 0, keepdims=True), 1, keepdims=True)
    exponent = jnp.ceil(jnp.log2(jnp.maximum(largest, 2.0**-100)))
    for out in (keep, pass_on):
        out[9] = jnp.broadcast_to(exponent, out.shape[1:])


def edge_part(links, me, own, received, other_in, on_in, off_in, first_k, second_k, first_acc, second_acc):
    rows_n, chans = own.shape[3:]
    cells = 4 * (rows_n + 16)
    return pl.pallas_call(
        edge_kernel,
        in_specs=[SMEM, SMEM] + [VMEM] * 9,
        out_specs=[VMEM] * 3,
        out_shape=[
            shape_of((10,) + first_acc.shape[1:], jnp.float32),
            shape_of((10,) + first_acc.shape[1:], jnp.float32),
            shape_of((cells, chans), jnp.float32),
        ],
        scratch_shapes=[
            pltpu.VMEM((2, 8, rows_n + 32, chans), jnp.float32),
            pltpu.VMEM((cells, 9 * chans), jnp.bfloat16),
            pltpu.VMEM((cells, 9 * chans), jnp.bfloat16),
            pltpu.VMEM((9 * chans, chans), jnp.bfloat16),
            pltpu.VMEM((9 * chans, chans), jnp.bfloat16),
        ],
        compiler_params=pltpu.CompilerParams(vmem_limit_bytes=8 * MIB),
        cost_estimate=pl.CostEstimate(flops=200 << 20, bytes_accessed=3 << 20, transcendentals=1 << 15),
        name="edge",
    )(links, me, own, received, other_in, on_in, off_in, first_k, second_k, first_acc, second_acc)


def state_kernel(grad, edge_grad, first_k, cot, out, g3, w_state):
    rows_n, cols_n, chans = cot.shape
    fill_paired(w_state, first_k, same_level(first_k.shape[2], chans), True)
    span = rows_n + 16
    x = lax.broadcasted_iota(jnp.int32, (cols_n, chans), 0)
    at_left, at_right = x == 0, x == cols_n - 1

    for row in range(rows_n + 2):
        at = rows_n if row == 0 else rows_n + 8 if row == rows_n + 1 else row - 1
        ends = [edge_grad[number * span + at : number * span + at + 1] for number in range(4)]
        values = grad[row // 2, row % 2].astype(jnp.float32)
        values = jnp.where(at_left, ends[1], jnp.where(at_right, ends[2], values))
        left = jnp.where(at_left, ends[0], pltpu.roll(values, 1, 0))
        right = jnp.where(at_right, ends[3], pltpu.roll(values, cols_n - 1, 0))
        for part, piece in enumerate((left, values, right)):
            g3[row // 2, row % 2, :, part * chans : (part + 1) * chans] = piece.astype(g3.dtype)
    for pair, count in spans_of(rows_n // 2, 4):
        back = dot(windows(g3, pair, count), w_state[...])
        for row in range(2):
            piece = back[:, row * chans : (row + 1) * chans].reshape(count, cols_n, chans)
            for k in range(count):
                y = 2 * (pair + k) + row
                out[y] = (cot[y].astype(jnp.float32) + piece[k]).astype(out.dtype)


def state_part(grad, edge_grad, first_k, cot):
    rows_n, cols_n, chans = cot.shape
    return pl.pallas_call(
        state_kernel,
        in_specs=[VMEM] * 4,
        out_specs=VMEM,
        out_shape=shape_of(cot.shape, jnp.bfloat16),
        scratch_shapes=[
            pltpu.VMEM((rows_n // 2 + 1, 2, cols_n, 3 * chans), jnp.bfloat16),
            pltpu.VMEM((12 * chans, 2 * chans), jnp.bfloat16),
        ],
        compiler_params=pltpu.CompilerParams(vmem_limit_bytes=12 * MIB),
        cost_estimate=pl.CostEstimate(flops=1200 << 20, bytes_accessed=3 << 20, transcendentals=0),
        name="state",
    )(grad, edge_grad, first_k, cot)


def exchanged(value, tiles, pairs):
    both = [(a, b) for a, b in pairs if a < tiles and b < tiles]
    return lax.ppermute(value, "tiles", both + [(b, a) for a, b in both])


STATE_AT = 2
TOP = 13.0


def power(k):
    bits = (k + 126.0).astype(jnp.int32)
    value = jnp.full_like(k, 2.0**-126)
    for bit in range(8):
        half = jnp.where(bits & (1 << bit) != 0, 2.0 ** min(1 << bit, 64), 1.0)
        value = value * half * (half if bit == 7 else 1.0)
    return value


def packed(total, exponent):
    values = (total * power(TOP - exponent)).astype(jnp.float16)
    return lax.optimization_barrier(jnp.concatenate([values, exponent.astype(jnp.float16)], 0))


def unpacked(packet):
    exponent = packet[9:].astype(jnp.float32)
    return packet[:9].astype(jnp.float32) * power(exponent - TOP), exponent


def summed(keep, pass_on, me, tiles, scale, edges, state_of):
    even = lax.rem(me, 2) == 0
    if tiles & (tiles - 1):
        first, second = jnp.where(even, keep, pass_on), jnp.where(even, pass_on, keep)
        first, second = lax.psum((first[:9], second[:9]), "tiles")
        return first * scale, second * scale, state_of(edges)
    on_chip = [(t, t + 1) for t in range(0, tiles, 2)]
    other = exchanged(pass_on, tiles, on_chip)
    total, exponent = keep[:9] + other[:9], jnp.maximum(keep[9:], other[9:]) + 1.0
    distance = 2
    while distance < tiles:
        here = distance == 2 if STATE_AT == 2 else 2 * distance >= tiles
        if here:
            total, edges = lax.optimization_barrier((total, edges))
        packet = packed(total, exponent)
        other = exchanged(packet, tiles, [(t, t + distance) for t in range(tiles) if not t & distance])
        if here:
            other, state_grad = lax.optimization_barrier((other, state_of(edges)))
        (total, exponent), (more, bound) = unpacked(packet), unpacked(other)
        total, exponent = total + more, jnp.maximum(exponent, bound) + 1.0
        distance *= 2
    total = total * scale
    other = exchanged(total, tiles, on_chip)
    return jnp.where(even, total, other), jnp.where(even, other, total), state_grad


def local(ocean_state, cotangent, first_kernel, second_kernel, neighbours):
    state, cot = ocean_state[0], cotangent[0]
    rows_n, cols_n, chans = state.shape
    tiles = lax.axis_size("tiles")
    index = lax.axis_index("tiles")
    me = jnp.reshape(index, (1,)).astype(jnp.int32)
    own, on_out, off_out = pack(neighbours, me, state, cot)
    on_chip = [(t, t + 1) for t in range(0, tiles, 2)]
    on_in = exchanged(on_out, tiles, on_chip)
    off_in = exchanged(off_out, tiles, [(t, t + 1) for t in range(1, tiles, 2)])
    cores = [list(range(core, tiles, 2)) for core in range(2)]
    sent = slots(tiles // 2, me, own, on_in)
    received = lax.all_to_all(sent, "tiles", 0, 0, axis_index_groups=cores)
    received = received.reshape((tiles,) + received.shape[2:])
    grad, first_acc, second_acc = main_part(
        neighbours, me, state, cot, on_in, off_in, first_kernel, second_kernel
    )
    received, first_acc = lax.optimization_barrier((received, first_acc))
    other_in = exchanged(received, tiles, on_chip)
    keep, pass_on, edge_grad = edge_part(
        neighbours, me, own, received, other_in, on_in, off_in, first_kernel, second_kernel, first_acc, second_acc
    )
    scale = 1.0 / math.sqrt(tiles * rows_n * cols_n)

    def state_of(edges):
        return state_part(grad, edges, first_kernel, cot)

    first, second, state_grad = summed(keep, pass_on, index, tiles, scale, edge_grad, state_of)
    shape = first_kernel.shape
    return state_grad[None], first.reshape(shape), second.reshape(shape)


def solution(mesh):
    placed = (
        P(("groups", "tiles"), None, None, None),
        P(("groups", "tiles"), None, None, None),
        P(),
        P(),
        P("tiles", None),
    )
    return jax.shard_map(
        local,
        mesh=mesh,
        in_specs=placed,
        out_specs=(
            P(("groups", "tiles"), None, None, None),
            P("groups", None, None, None),
            P("groups", None, None, None),
        ),
        check_vma=False,
    )
```

```python
import functools
import math

import jax
import jax.numpy as jnp
from jax import lax
from jax.experimental import pallas as pl
from jax.experimental.pallas import tpu as pltpu
from jax.sharding import PartitionSpec as P

CUBE = 0.044715
ROOT = math.sqrt(2.0 / math.pi)
MIB = 1 << 20
PACK = 8
SMEM = pl.BlockSpec(memory_space=pltpu.SMEM)
VMEM = pl.BlockSpec(memory_space=pltpu.VMEM)


def shape_of(dims, dtype):
    return jax.ShapeDtypeStruct(dims, dtype)


def partners(me):
    odd = lax.rem(me, 2)
    return me + 1 - 2 * odd, me - 1 + 2 * odd


def gelu_pair(v):
    square = v * v
    t = jnp.tanh(ROOT * v * (1.0 + CUBE * square))
    half = 0.5 * (1.0 + t)
    slope = half + (0.5 * ROOT) * v * (1.0 - t * t) * (1.0 + (3.0 * CUBE) * square)
    return v * half, slope


def pack_kernel(
    chips, links_in, me_ref, state, cot,
    own, send, on_out, off_out, rows, columns, links, sem, links_sem, send_sem,
):
    rows_n, cols_n, chans = state.shape
    me = me_ref[0]
    copies = [pltpu.make_async_copy(links_in, links, links_sem)]
    for f, field in enumerate((state, cot)):
        for side in range(2):
            beside = field.at[:, pl.ds(side * (cols_n - 16), 16)]
            copies.append(pltpu.make_async_copy(beside, columns.at[f, side], sem.at[f, side]))
            outer = field.at[pl.ds(side * (rows_n - 2), 2)]
            copies.append(pltpu.make_async_copy(outer, rows.at[f, side], sem.at[f, 2 + side]))
    for copy in copies:
        copy.start()
    for copy in copies:
        copy.wait()
    for f in range(2):
        for side, first in ((0, 0), (1, 14)):
            values = columns[f, side].astype(jnp.float32)
            for c in range(2):
                own[side, f, c] = values[:, first + c, :].astype(jnp.bfloat16)
    copies = []
    for j in range(chips):
        side = jnp.where(2 * j + 1 > me, 1, 0)
        copies.append(pltpu.make_async_copy(own.at[side], send.at[j], send_sem.at[j]))
        copies[-1].start()
    for target, out in zip(partners(me), (on_out, off_out)):
        for f in range(2):
            top, bottom = rows[f, 0], rows[f, 1]
            sent = jnp.where(links[0, 1] == target, bottom, jnp.zeros_like(bottom))
            out[2 * f : 2 * f + 2] = jnp.where(links[0, 0] == target, top, sent)
    for copy in copies:
        copy.wait()


def pack(chips, links, me, state, cot):
    rows_n, cols_n, chans = state.shape
    far = pl.BlockSpec(memory_space=pltpu.HBM)
    placed = functools.partial(pltpu.with_memory_space_constraint, memory_space=pltpu.HBM)
    return pl.pallas_call(
        functools.partial(pack_kernel, chips),
        in_specs=[far, SMEM, far, far],
        out_specs=[VMEM, far, VMEM, VMEM],
        out_shape=[
            shape_of((2, 2, 2, rows_n, chans), jnp.bfloat16),
            pltpu.HBM((chips, 2, 2, rows_n, chans), jnp.bfloat16),
            shape_of((4, cols_n, chans), jnp.bfloat16),
            shape_of((4, cols_n, chans), jnp.bfloat16),
        ],
        scratch_shapes=[
            pltpu.VMEM((2, 2, 2, cols_n, chans), jnp.bfloat16),
            pltpu.VMEM((2, 2, rows_n, 16, chans), jnp.bfloat16),
            pltpu.SMEM(links.shape, links.dtype),
            pltpu.SemaphoreType.DMA((2, 4)),
            pltpu.SemaphoreType.DMA,
            pltpu.SemaphoreType.DMA((chips,)),
        ],
        compiler_params=pltpu.CompilerParams(vmem_limit_bytes=PACK * MIB),
        name="pack",
    )(placed(links), me, placed(state), placed(cot))


def halo_rows(links, me, on_in, off_in, f):
    found = []
    for link in (0, 1):
        rows = jnp.zeros((2,) + off_in.shape[1:], off_in.dtype)
        for source, packet in zip(partners(me), (on_in, off_in)):
            rows = jnp.where(links[0, link] == source, packet[2 * f : 2 * f + 2], rows)
        found.append(rows)
    return found


def same_level(width, chans):
    down = lax.broadcasted_iota(jnp.int32, (chans, chans), 0) // width
    across = lax.broadcasted_iota(jnp.int32, (chans, chans), 1) // width
    return down == across


def diagonal(product, mask, width):
    kept = jnp.where(mask, product, 0.0)
    return sum(kept[at : at + width] for at in range(0, product.shape[0], width))


def thirds(ref, row, values):
    count, cols_n, chans = values.shape
    flat = values.reshape(count * cols_n, chans).astype(jnp.float32)
    left = pltpu.roll(flat, 1, 0).astype(ref.dtype)
    right = pltpu.roll(flat, count * cols_n - 1, 0).astype(ref.dtype)
    for part, piece in enumerate((left, values, right)):
        lanes = slice(part * chans, (part + 1) * chans)
        ref[pl.ds(row // 2, count // 2), :, :, lanes] = piece.reshape(count // 2, 2, cols_n, chans)


def windows(ref, pair, count):
    parts = []
    for row in range(4):
        rows = ref[pl.ds(pair + row // 2, count), row % 2]
        parts.append(rows.reshape(count * rows.shape[1], rows.shape[2]))
    return jnp.concatenate(parts, 1)


def dot(a, b):
    return jnp.dot(a, b, preferred_element_type=jnp.float32)


def spans_of(total, most):
    count = pl.cdiv(total, most)
    bounds = [total * i // count for i in range(count + 1)]
    return [(lo, hi - lo) for lo, hi in zip(bounds, bounds[1:])]


def level_blocks(kernel, tap, mask):
    block = kernel[tap // 3, tap % 3].astype(jnp.float32)
    return jnp.where(mask, jnp.concatenate([block] * (mask.shape[0] // block.shape[0]), 0), 0.0)


def fill_paired(ref, kernel, mask, turned):
    chans = mask.shape[0]
    none = jnp.zeros((3 * chans, chans), ref.dtype)
    ref[9 * chans : 12 * chans, 0:chans] = none
    ref[0 : 3 * chans, chans : 2 * chans] = none
    for tap in range(9):
        dense = level_blocks(kernel, tap, mask)
        if turned:
            paired(ref, 8 - tap, dense.T.astype(ref.dtype))
        else:
            paired(ref, tap, dense.astype(ref.dtype))


def paired(ref, tap, dense):
    chans = dense.shape[0]
    for row in range(2):
        ref[pl.ds((tap + 3 * row) * chans, chans), row * chans : (row + 1) * chans] = dense


def main_kernel(
    links, me_ref, state, cot, on_in, off_in, first_k, second_k,
    grad, first_acc, second_acc,
    w_pre, w_back, s3, c3, acc1, acc2, grad_v, sem,
):
    me = me_ref[0]
    rows_n, cols_n, chans = state.shape
    width = first_k.shape[2]
    mask = same_level(width, chans)
    fill_paired(w_pre, first_k, mask, False)
    fill_paired(w_back, second_k, mask, True)
    for f, (field, store) in enumerate(((state, s3), (cot, c3))):
        above, below = halo_rows(links, me, on_in, off_in, f)
        thirds(store, 0, above)
        thirds(store, rows_n + 2, below)
        for row, count in spans_of(rows_n // 2, 4):
            thirds(store, 2 * row + 2, field[pl.ds(2 * row, 2 * count)])

    acc1[...] = jnp.zeros_like(acc1)
    acc2[...] = jnp.zeros_like(acc2)
    pairs_n = rows_n // 2 + 1
    copies = []
    for k, (pair, count) in enumerate(spans_of(pairs_n, PAIRS)):
        near_state, near_cot = windows(s3, pair, count), windows(c3, pair, count)
        hidden, slope = gelu_pair(dot(near_state, w_pre[...]))
        grads = dot(near_cot, w_back[...]) * slope
        cell = lax.broadcasted_iota(jnp.int32, grads.shape, 0)
        lane = lax.broadcasted_iota(jnp.int32, grads.shape, 1)
        x = lax.rem(cell, cols_n)
        inner = (x > 0) & (x < cols_n - 1)
        if pair == 0:
            outside = (cell < cols_n) & (lane < chans)
            inner = inner & ~outside
            grads = jnp.where(outside & (links[0, 0] < 0), 0.0, grads)
        if pair + count == pairs_n:
            outside = (cell >= (count - 1) * cols_n) & (lane >= chans)
            inner = inner & ~outside
            grads = jnp.where(outside & (links[0, 1] < 0), 0.0, grads)
        for row in range(2):
            piece = grads[:, row * chans : (row + 1) * chans].astype(jnp.bfloat16)
            grad_v[pl.ds(pair, count), row] = piece.reshape(count, cols_n, chans)
        part = pl.ds(pair, count)
        copies.append(pltpu.make_async_copy(grad_v.at[part], grad.at[part], sem.at[k]))
        copies[-1].start()
        grads = jnp.where(inner, grads, 0.0).astype(jnp.bfloat16)
        hidden = jnp.where(inner, hidden, 0.0).astype(jnp.bfloat16)
        acc1[...] += dot(grads.T, near_state)
        acc2[...] += dot(hidden.T, near_cot)
    for tap in range(9):
        one, two = (slice((tap + 3 * r) * chans, (tap + 3 * r + 1) * chans) for r in range(2))
        first = acc1[0:chans, one] + acc1[chans : 2 * chans, two]
        second = acc2[0:chans, one] + acc2[chans : 2 * chans, two]
        first_acc[tap] = diagonal(first.T, mask, width)
        second_acc[8 - tap] = diagonal(second, mask, width)
    for copy in copies:
        copy.wait()


PAIRS = 9


def main_part(links, me, state, cot, on_in, off_in, first_k, second_k):
    rows_n, cols_n, chans = state.shape
    width = first_k.shape[2]
    flops = 2 * rows_n * cols_n * 9 * chans * chans * 4
    return pl.pallas_call(
        main_kernel,
        in_specs=[SMEM, SMEM] + [VMEM] * 6,
        out_specs=[pl.BlockSpec(memory_space=pltpu.HBM), VMEM, VMEM],
        out_shape=[
            pltpu.HBM((rows_n // 2 + 1, 2, cols_n, chans), jnp.bfloat16),
            shape_of((9, width, chans), jnp.float32),
            shape_of((9, width, chans), jnp.float32),
        ],
        scratch_shapes=[
            pltpu.VMEM((12 * chans, 2 * chans), jnp.bfloat16),
            pltpu.VMEM((12 * chans, 2 * chans), jnp.bfloat16),
            pltpu.VMEM((rows_n // 2 + 2, 2, cols_n, 3 * chans), jnp.bfloat16),
            pltpu.VMEM((rows_n // 2 + 2, 2, cols_n, 3 * chans), jnp.bfloat16),
            pltpu.VMEM((2 * chans, 12 * chans), jnp.float32),
            pltpu.VMEM((2 * chans, 12 * chans), jnp.float32),
            pltpu.VMEM((rows_n // 2 + 1, 2, cols_n, chans), jnp.bfloat16),
            pltpu.SemaphoreType.DMA((len(spans_of(rows_n // 2 + 1, PAIRS)),)),
        ],
        compiler_params=pltpu.CompilerParams(vmem_limit_bytes=26 * MIB),
        cost_estimate=pl.CostEstimate(flops=20 * flops, bytes_accessed=5 << 20, transcendentals=1 << 19),
        name="main",
    )(links, me, state, cot, on_in, off_in, first_k, second_k)


BASE = 16


def edge_kernel(
    links, me_ref, own, received, other_in, on_in, off_in, first_k, second_k, first_acc, second_acc,
    keep, pass_on, edge_grad, store, lhs_s, lhs_c, w_pre, w_back,
):
    me = me_ref[0]
    rows_n, chans = own.shape[3], own.shape[4]
    cols_n = off_in.shape[1]
    width = first_acc.shape[1]
    span = rows_n + 16
    mask = same_level(width, chans)
    for tap in range(9):
        at = slice(tap * chans, (tap + 1) * chans)
        w_pre[at] = level_blocks(first_k, tap, mask).astype(w_pre.dtype)
        w_back[at] = level_blocks(second_k, 8 - tap, mask).T.astype(w_back.dtype)
    store[...] = jnp.zeros_like(store)
    low, high = pl.ds(BASE - 2, 2), pl.ds(BASE + rows_n, 2)
    for f in range(2):
        rows = halo_rows(links, me, on_in, off_in, f)
        for side, link, over, under in ((0, 2, 4, 6), (1, 3, 5, 7)):
            outer, mine = (0, 2) if side == 0 else (6, 4)

            def sent(entry):
                tile = links[0, entry]
                at = jnp.maximum(tile, 0)
                chip, same = at // 2, lax.rem(at, 2) == lax.rem(me, 2)
                piece = jnp.where(same, received[chip, f], other_in[chip, f]).astype(jnp.float32)
                return jnp.where(tile >= 0, piece, 0.0)

            beside, corner_over, corner_under = sent(link), sent(over), sent(under)
            for c in range(2):
                store[f, mine + c, pl.ds(BASE, rows_n)] = own[side, f, c].astype(jnp.float32)
                store[f, outer + c, pl.ds(BASE, rows_n)] = beside[c]
                store[f, outer + c, low] = corner_over[c, rows_n - 2 : rows_n]
                store[f, outer + c, high] = corner_under[c, 0:2]
            at = 0 if side == 0 else cols_n - 16
            first = 0 if side == 0 else 14
            for where, halo in ((BASE - 2, rows[0]), (BASE + rows_n, rows[1])):
                edge = halo[:, at : at + 16].astype(jnp.float32)
                for r in range(2):
                    for c in range(2):
                        store[f, mine + c, pl.ds(where + r, 1)] = edge[r, first + c : first + c + 1]
        target = (lhs_s, lhs_c)[f]
        for column, base in enumerate((0, 1, 4, 5)):
            for a in range(3):
                for b in range(3):
                    lanes = pl.ds((3 * a + b) * chans, chans)
                    column_in = store.at[f, base + b]
                    target[pl.ds(column * span, rows_n), lanes] = column_in[
                        pl.ds(BASE - 1 + a, rows_n)
                    ].astype(jnp.bfloat16)
                    ends = [column_in[pl.ds(BASE - 2 + a, 8)], column_in[pl.ds(BASE + rows_n - 1 + a, 8)]]
                    target[pl.ds(column * span + rows_n, 16), lanes] = jnp.concatenate(ends, 0).astype(
                        jnp.bfloat16
                    )
    hidden, slope = gelu_pair(dot(lhs_s[...], w_pre[...]))
    grads = dot(lhs_c[...], w_back[...]) * slope
    valid = ((2, 4, 6), (None, 0, 1), (None, 0, 1), (3, 5, 7))
    for column in range(4):
        spans = ((0, rows_n), (rows_n, 8), (rows_n + 8, 8))
        for entry, (start, count) in zip(valid[column], spans):
            start += column * span
            piece = grads[start : start + count]
            if entry is not None:
                piece = jnp.where(links[0, entry] >= 0, piece, 0.0)
            edge_grad[pl.ds(start, count)] = piece.astype(jnp.bfloat16).astype(jnp.float32)

    def inner(values):
        return jnp.concatenate([values[span : span + rows_n], values[2 * span : 2 * span + rows_n]], 0)

    def inner_of(ref):
        return jnp.concatenate([ref[pl.ds(span, rows_n)], ref[pl.ds(2 * span, rows_n)]], 0)

    def over_cells(a, b):
        return lax.dot_general(a, b, (((0,), (0,)), ((), ())), preferred_element_type=jnp.float32)

    first_p = over_cells(inner_of(lhs_s), inner(grads).astype(jnp.bfloat16))
    second_p = over_cells(inner(hidden).astype(jnp.bfloat16), inner_of(lhs_c))
    even = lax.rem(me, 2) == 0
    for tap in range(9):
        part = slice(tap * chans, (tap + 1) * chans)
        first = first_acc[tap] + diagonal(first_p[part], mask, width)
        turned = slice((8 - tap) * chans, (9 - tap) * chans)
        second = second_acc[tap] + diagonal(second_p[:, turned], mask, width)
        keep[tap] = jnp.where(even, first, second)
        pass_on[tap] = jnp.where(even, second, first)
        size = jnp.maximum(jnp.abs(first), jnp.abs(second))
        largest = size if tap == 0 else jnp.maximum(largest, size)
    largest = jnp.max(jnp.max(largest, 0, keepdims=True), 1, keepdims=True)
    exponent = jnp.ceil(jnp.log2(jnp.maximum(largest, 2.0**-100)))
    for out in (keep, pass_on):
        out[9] = jnp.broadcast_to(exponent, out.shape[1:])


def edge_part(links, me, own, received, other_in, on_in, off_in, first_k, second_k, first_acc, second_acc):
    rows_n, chans = own.shape[3:]
    cells = 4 * (rows_n + 16)
    return pl.pallas_call(
        edge_kernel,
        in_specs=[SMEM, SMEM] + [VMEM] * 9,
        out_specs=[VMEM] * 3,
        out_shape=[
            shape_of((10,) + first_acc.shape[1:], jnp.float32),
            shape_of((10,) + first_acc.shape[1:], jnp.float32),
            shape_of((cells, chans), jnp.float32),
        ],
        scratch_shapes=[
            pltpu.VMEM((2, 8, rows_n + 32, chans), jnp.float32),
            pltpu.VMEM((cells, 9 * chans), jnp.bfloat16),
            pltpu.VMEM((cells, 9 * chans), jnp.bfloat16),
            pltpu.VMEM((9 * chans, chans), jnp.bfloat16),
            pltpu.VMEM((9 * chans, chans), jnp.bfloat16),
        ],
        compiler_params=pltpu.CompilerParams(vmem_limit_bytes=8 * MIB),
        cost_estimate=pl.CostEstimate(flops=200 << 20, bytes_accessed=3 << 20, transcendentals=1 << 15),
        name="edge",
    )(links, me, own, received, other_in, on_in, off_in, first_k, second_k, first_acc, second_acc)


def state_kernel(grad, edge_grad, first_k, cot, out, g3, w_state):
    rows_n, cols_n, chans = cot.shape
    fill_paired(w_state, first_k, same_level(first_k.shape[2], chans), True)
    span = rows_n + 16
    x = lax.broadcasted_iota(jnp.int32, (cols_n, chans), 0)
    at_left, at_right = x == 0, x == cols_n - 1

    for row in range(rows_n + 2):
        at = rows_n if row == 0 else rows_n + 8 if row == rows_n + 1 else row - 1
        ends = [edge_grad[number * span + at : number * span + at + 1] for number in range(4)]
        values = grad[row // 2, row % 2].astype(jnp.float32)
        values = jnp.where(at_left, ends[1], jnp.where(at_right, ends[2], values))
        left = jnp.where(at_left, ends[0], pltpu.roll(values, 1, 0))
        right = jnp.where(at_right, ends[3], pltpu.roll(values, cols_n - 1, 0))
        for part, piece in enumerate((left, values, right)):
            g3[row // 2, row % 2, :, part * chans : (part + 1) * chans] = piece.astype(g3.dtype)
    for pair, count in spans_of(rows_n // 2, 4):
        back = dot(windows(g3, pair, count), w_state[...])
        for row in range(2):
            piece = back[:, row * chans : (row + 1) * chans].reshape(count, cols_n, chans)
            for k in range(count):
                y = 2 * (pair + k) + row
                out[y] = (cot[y].astype(jnp.float32) + piece[k]).astype(out.dtype)


def state_part(grad, edge_grad, first_k, cot):
    rows_n, cols_n, chans = cot.shape
    return pl.pallas_call(
        state_kernel,
        in_specs=[VMEM] * 4,
        out_specs=VMEM,
        out_shape=shape_of(cot.shape, jnp.bfloat16),
        scratch_shapes=[
            pltpu.VMEM((rows_n // 2 + 1, 2, cols_n, 3 * chans), jnp.bfloat16),
            pltpu.VMEM((12 * chans, 2 * chans), jnp.bfloat16),
        ],
        compiler_params=pltpu.CompilerParams(vmem_limit_bytes=12 * MIB),
        cost_estimate=pl.CostEstimate(flops=1200 << 20, bytes_accessed=3 << 20, transcendentals=0),
        name="state",
    )(grad, edge_grad, first_k, cot)


def exchanged(value, tiles, pairs):
    both = [(a, b) for a, b in pairs if a < tiles and b < tiles]
    return lax.ppermute(value, "tiles", both + [(b, a) for a, b in both])


STATE_AT = 2
TOP = 13.0


def power(k):
    bits = (k + 126.0).astype(jnp.int32)
    value = jnp.full_like(k, 2.0**-126)
    for bit in range(8):
        half = jnp.where(bits & (1 << bit) != 0, 2.0 ** min(1 << bit, 64), 1.0)
        value = value * half * (half if bit == 7 else 1.0)
    return value


def packed(total, exponent):
    values = (total * power(TOP - exponent)).astype(jnp.float16)
    return lax.optimization_barrier(jnp.concatenate([values, exponent.astype(jnp.float16)], 0))


def unpacked(packet):
    exponent = packet[9:].astype(jnp.float32)
    return packet[:9].astype(jnp.float32) * power(exponent - TOP), exponent


def summed(keep, pass_on, me, tiles, scale, edges, state_of):
    even = lax.rem(me, 2) == 0
    if tiles & (tiles - 1):
        first, second = jnp.where(even, keep, pass_on), jnp.where(even, pass_on, keep)
        first, second = lax.psum((first[:9], second[:9]), "tiles")
        return first * scale, second * scale, state_of(edges)
    on_chip = [(t, t + 1) for t in range(0, tiles, 2)]
    other = exchanged(pass_on, tiles, on_chip)
    total, exponent = keep[:9] + other[:9], jnp.maximum(keep[9:], other[9:]) + 1.0
    distance = 2
    while distance < tiles:
        here = distance == 2 if STATE_AT == 2 else 2 * distance >= tiles
        if here:
            total, edges = lax.optimization_barrier((total, edges))
        packet = packed(total, exponent)
        other = exchanged(packet, tiles, [(t, t + distance) for t in range(tiles) if not t & distance])
        if here:
            other, state_grad = lax.optimization_barrier((other, state_of(edges)))
        (total, exponent), (more, bound) = unpacked(packet), unpacked(other)
        total, exponent = total + more, jnp.maximum(exponent, bound) + 1.0
        distance *= 2
    total = total * scale
    other = exchanged(total, tiles, on_chip)
    return jnp.where(even, total, other), jnp.where(even, other, total), state_grad


def local(ocean_state, cotangent, first_kernel, second_kernel, neighbours):
    state, cot = ocean_state[0], cotangent[0]
    rows_n, cols_n, chans = state.shape
    tiles = lax.axis_size("tiles")
    index = lax.axis_index("tiles")
    me = jnp.reshape(index, (1,)).astype(jnp.int32)
    own, send, on_out, off_out = pack(tiles // 2, neighbours, me, state, cot)
    on_chip = [(t, t + 1) for t in range(0, tiles, 2)]
    on_in = exchanged(on_out, tiles, on_chip)
    off_in = exchanged(off_out, tiles, [(t, t + 1) for t in range(1, tiles, 2)])
    cores = [list(range(core, tiles, 2)) for core in range(2)]
    received = lax.all_to_all(send, "tiles", 0, 0, axis_index_groups=cores)
    grad, first_acc, second_acc = main_part(
        neighbours, me, state, cot, on_in, off_in, first_kernel, second_kernel
    )
    received, first_acc = lax.optimization_barrier((received, first_acc))
    other_in = exchanged(received, tiles, on_chip)
    keep, pass_on, edge_grad = edge_part(
        neighbours, me, own, received, other_in, on_in, off_in, first_kernel, second_kernel, first_acc, second_acc
    )
    scale = 1.0 / math.sqrt(tiles * rows_n * cols_n)

    def state_of(edges):
        return state_part(grad, edges, first_kernel, cot)

    first, second, state_grad = summed(keep, pass_on, index, tiles, scale, edge_grad, state_of)
    shape = first_kernel.shape
    return state_grad[None], first.reshape(shape), second.reshape(shape)


def solution(mesh):
    placed = (
        P(("groups", "tiles"), None, None, None),
        P(("groups", "tiles"), None, None, None),
        P(),
        P(),
        P("tiles", None),
    )
    return jax.shard_map(
        local,
        mesh=mesh,
        in_specs=placed,
        out_specs=(
            P(("groups", "tiles"), None, None, None),
            P("groups", None, None, None),
            P("groups", None, None, None),
        ),
        check_vma=False,
    )
```

```python
import functools
import math

import jax
import jax.numpy as jnp
from jax import lax
from jax.experimental import pallas as pl
from jax.experimental.pallas import tpu as pltpu
from jax.sharding import PartitionSpec as P

CUBE = 0.044715
ROOT = math.sqrt(2.0 / math.pi)
MIB = 1 << 20
PACK = 8
SMEM = pl.BlockSpec(memory_space=pltpu.SMEM)
VMEM = pl.BlockSpec(memory_space=pltpu.VMEM)


def shape_of(dims, dtype):
    return jax.ShapeDtypeStruct(dims, dtype)


def partners(me):
    odd = lax.rem(me, 2)
    return me + 1 - 2 * odd, me - 1 + 2 * odd


def gelu_pair(v):
    square = v * v
    t = jnp.tanh(ROOT * v * (1.0 + CUBE * square))
    half = 0.5 * (1.0 + t)
    slope = half + (0.5 * ROOT) * v * (1.0 - t * t) * (1.0 + (3.0 * CUBE) * square)
    return v * half, slope


def pack_kernel(
    chips, links_in, me_ref, state, cot,
    own, send, on_out, off_out, rows, columns, links, sem, links_sem, send_sem,
):
    rows_n, cols_n, chans = state.shape
    me = me_ref[0]
    copies = [pltpu.make_async_copy(links_in, links, links_sem)]
    for f, field in enumerate((state, cot)):
        for side in range(2):
            beside = field.at[:, pl.ds(side * (cols_n - 16), 16)]
            copies.append(pltpu.make_async_copy(beside, columns.at[f, side], sem.at[f, side]))
            outer = field.at[pl.ds(side * (rows_n - 2), 2)]
            copies.append(pltpu.make_async_copy(outer, rows.at[f, side], sem.at[f, 2 + side]))
    for copy in copies:
        copy.start()
    for copy in copies:
        copy.wait()
    for f in range(2):
        for side, first in ((0, 0), (1, 14)):
            values = columns[f, side].astype(jnp.float32)
            for c in range(2):
                own[side, f, c] = values[:, first + c, :].astype(jnp.bfloat16)
    copies = []
    for j in range(chips):
        side = jnp.where(2 * j + 1 > me, 1, 0)
        copies.append(pltpu.make_async_copy(own.at[side], send.at[j], send_sem.at[j]))
        copies[-1].start()
    for target, out in zip(partners(me), (on_out, off_out)):
        for f in range(2):
            top, bottom = rows[f, 0], rows[f, 1]
            sent = jnp.where(links[0, 1] == target, bottom, jnp.zeros_like(bottom))
            out[2 * f : 2 * f + 2] = jnp.where(links[0, 0] == target, top, sent)
    for copy in copies:
        copy.wait()


def pack(chips, links, me, state, cot):
    rows_n, cols_n, chans = state.shape
    far = pl.BlockSpec(memory_space=pltpu.HBM)
    placed = functools.partial(pltpu.with_memory_space_constraint, memory_space=pltpu.HBM)
    return pl.pallas_call(
        functools.partial(pack_kernel, chips),
        in_specs=[far, SMEM, far, far],
        out_specs=[VMEM, far, VMEM, VMEM],
        out_shape=[
            shape_of((2, 2, 2, rows_n, chans), jnp.bfloat16),
            pltpu.HBM((chips, 2, 2, rows_n, chans), jnp.bfloat16),
            shape_of((4, cols_n, chans), jnp.bfloat16),
            shape_of((4, cols_n, chans), jnp.bfloat16),
        ],
        scratch_shapes=[
            pltpu.VMEM((2, 2, 2, cols_n, chans), jnp.bfloat16),
            pltpu.VMEM((2, 2, rows_n, 16, chans), jnp.bfloat16),
            pltpu.SMEM(links.shape, links.dtype),
            pltpu.SemaphoreType.DMA((2, 4)),
            pltpu.SemaphoreType.DMA,
            pltpu.SemaphoreType.DMA((chips,)),
        ],
        compiler_params=pltpu.CompilerParams(vmem_limit_bytes=PACK * MIB),
        name="pack",
    )(placed(links), me, placed(state), placed(cot))


def halo_rows(links, me, on_in, off_in, f):
    found = []
    for link in (0, 1):
        rows = jnp.zeros((2,) + off_in.shape[1:], off_in.dtype)
        for source, packet in zip(partners(me), (on_in, off_in)):
            rows = jnp.where(links[0, link] == source, packet[2 * f : 2 * f + 2], rows)
        found.append(rows)
    return found


def same_level(width, chans):
    down = lax.broadcasted_iota(jnp.int32, (chans, chans), 0) // width
    across = lax.broadcasted_iota(jnp.int32, (chans, chans), 1) // width
    return down == across


def diagonal(product, mask, width):
    kept = jnp.where(mask, product, 0.0)
    return sum(kept[at : at + width] for at in range(0, product.shape[0], width))


def thirds(ref, row, values):
    count, cols_n, chans = values.shape
    flat = values.reshape(count * cols_n, chans).astype(jnp.float32)
    left = pltpu.roll(flat, 1, 0).astype(ref.dtype)
    right = pltpu.roll(flat, count * cols_n - 1, 0).astype(ref.dtype)
    for part, piece in enumerate((left, values, right)):
        lanes = slice(part * chans, (part + 1) * chans)
        ref[pl.ds(row // 2, count // 2), :, :, lanes] = piece.reshape(count // 2, 2, cols_n, chans)


def windows(ref, pair, count):
    parts = []
    for row in range(4):
        rows = ref[pl.ds(pair + row // 2, count), row % 2]
        parts.append(rows.reshape(count * rows.shape[1], rows.shape[2]))
    return jnp.concatenate(parts, 1)


def dot(a, b):
    return jnp.dot(a, b, preferred_element_type=jnp.float32)


def spans_of(total, most):
    count = pl.cdiv(total, most)
    bounds = [total * i // count for i in range(count + 1)]
    return [(lo, hi - lo) for lo, hi in zip(bounds, bounds[1:])]


def level_blocks(kernel, tap, mask):
    block = kernel[tap // 3, tap % 3].astype(jnp.float32)
    return jnp.where(mask, jnp.concatenate([block] * (mask.shape[0] // block.shape[0]), 0), 0.0)


def fill_paired(ref, kernel, mask, turned):
    chans = mask.shape[0]
    none = jnp.zeros((3 * chans, chans), ref.dtype)
    ref[9 * chans : 12 * chans, 0:chans] = none
    ref[0 : 3 * chans, chans : 2 * chans] = none
    for tap in range(9):
        dense = level_blocks(kernel, tap, mask)
        if turned:
            paired(ref, 8 - tap, dense.T.astype(ref.dtype))
        else:
            paired(ref, tap, dense.astype(ref.dtype))


def paired(ref, tap, dense):
    chans = dense.shape[0]
    for row in range(2):
        ref[pl.ds((tap + 3 * row) * chans, chans), row * chans : (row + 1) * chans] = dense


def main_kernel(
    links, me_ref, state, cot, on_in, off_in, first_k, second_k,
    grad, first_acc, second_acc,
    w_pre, w_back, s3, c3, acc1, acc2, grad_v, sem,
):
    me = me_ref[0]
    rows_n, cols_n, chans = state.shape
    width = first_k.shape[2]
    mask = same_level(width, chans)
    fill_paired(w_pre, first_k, mask, False)
    fill_paired(w_back, second_k, mask, True)
    for f, (field, store) in enumerate(((state, s3), (cot, c3))):
        above, below = halo_rows(links, me, on_in, off_in, f)
        thirds(store, 0, above)
        thirds(store, rows_n + 2, below)
        for row, count in spans_of(rows_n // 2, 4):
            thirds(store, 2 * row + 2, field[pl.ds(2 * row, 2 * count)])

    pairs_n = rows_n // 2 + 1
    def products(pair, grads, hidden, near_state, near_cot):
        one, two = dot(grads.T, near_state), dot(hidden.T, near_cot)
        if pair == 0:
            acc1[...] = one
            acc2[...] = two
        else:
            acc1[...] += one
            acc2[...] += two

    copies = []
    later = None
    for k, (pair, count) in enumerate(spans_of(pairs_n, PAIRS)):
        near_state, near_cot = windows(s3, pair, count), windows(c3, pair, count)
        pre, back = dot(near_state, w_pre[...]), dot(near_cot, w_back[...])
        if later is not None:
            products(*later)
        hidden, slope = gelu_pair(pre)
        grads = back * slope
        cell = lax.broadcasted_iota(jnp.int32, grads.shape, 0)
        lane = lax.broadcasted_iota(jnp.int32, grads.shape, 1)
        x = lax.rem(cell, cols_n)
        inner = (x > 0) & (x < cols_n - 1)
        if pair == 0:
            outside = (cell < cols_n) & (lane < chans)
            inner = inner & ~outside
            grads = jnp.where(outside & (links[0, 0] < 0), 0.0, grads)
        if pair + count == pairs_n:
            outside = (cell >= (count - 1) * cols_n) & (lane >= chans)
            inner = inner & ~outside
            grads = jnp.where(outside & (links[0, 1] < 0), 0.0, grads)
        for row in range(2):
            piece = grads[:, row * chans : (row + 1) * chans].astype(jnp.bfloat16)
            grad_v[pl.ds(pair, count), row] = piece.reshape(count, cols_n, chans)
        part = pl.ds(pair, count)
        copies.append(pltpu.make_async_copy(grad_v.at[part], grad.at[part], sem.at[k]))
        copies[-1].start()
        grads = jnp.where(inner, grads, 0.0).astype(jnp.bfloat16)
        hidden = jnp.where(inner, hidden, 0.0).astype(jnp.bfloat16)
        later = (pair, grads, hidden, near_state, near_cot)
    products(*later)
    for tap in range(9):
        one, two = (slice((tap + 3 * r) * chans, (tap + 3 * r + 1) * chans) for r in range(2))
        first = acc1[0:chans, one] + acc1[chans : 2 * chans, two]
        second = acc2[0:chans, one] + acc2[chans : 2 * chans, two]
        first_acc[tap] = diagonal(first.T, mask, width)
        second_acc[8 - tap] = diagonal(second, mask, width)
    for copy in copies:
        copy.wait()


PAIRS = 6


def main_part(links, me, state, cot, on_in, off_in, first_k, second_k):
    rows_n, cols_n, chans = state.shape
    width = first_k.shape[2]
    flops = 2 * rows_n * cols_n * 9 * chans * chans * 4
    return pl.pallas_call(
        main_kernel,
        in_specs=[SMEM, SMEM] + [VMEM] * 6,
        out_specs=[pl.BlockSpec(memory_space=pltpu.HBM), VMEM, VMEM],
        out_shape=[
            pltpu.HBM((rows_n // 2 + 1, 2, cols_n, chans), jnp.bfloat16),
            shape_of((9, width, chans), jnp.float32),
            shape_of((9, width, chans), jnp.float32),
        ],
        scratch_shapes=[
            pltpu.VMEM((12 * chans, 2 * chans), jnp.bfloat16),
            pltpu.VMEM((12 * chans, 2 * chans), jnp.bfloat16),
            pltpu.VMEM((rows_n // 2 + 2, 2, cols_n, 3 * chans), jnp.bfloat16),
            pltpu.VMEM((rows_n // 2 + 2, 2, cols_n, 3 * chans), jnp.bfloat16),
            pltpu.VMEM((2 * chans, 12 * chans), jnp.float32),
            pltpu.VMEM((2 * chans, 12 * chans), jnp.float32),
            pltpu.VMEM((rows_n // 2 + 1, 2, cols_n, chans), jnp.bfloat16),
            pltpu.SemaphoreType.DMA((len(spans_of(rows_n // 2 + 1, PAIRS)),)),
        ],
        compiler_params=pltpu.CompilerParams(vmem_limit_bytes=26 * MIB),
        cost_estimate=pl.CostEstimate(flops=20 * flops, bytes_accessed=5 << 20, transcendentals=1 << 19),
        name="main",
    )(links, me, state, cot, on_in, off_in, first_k, second_k)


BASE = 16


def edge_kernel(
    links, me_ref, own, received, other_in, on_in, off_in, first_k, second_k, first_acc, second_acc,
    keep, pass_on, edge_grad, store, lhs_s, lhs_c, w_pre, w_back,
):
    me = me_ref[0]
    rows_n, chans = own.shape[3], own.shape[4]
    cols_n = off_in.shape[1]
    width = first_acc.shape[1]
    span = rows_n + 16
    mask = same_level(width, chans)
    for tap in range(9):
        at = slice(tap * chans, (tap + 1) * chans)
        w_pre[at] = level_blocks(first_k, tap, mask).astype(w_pre.dtype)
        w_back[at] = level_blocks(second_k, 8 - tap, mask).T.astype(w_back.dtype)
    store[...] = jnp.zeros_like(store)
    low, high = pl.ds(BASE - 2, 2), pl.ds(BASE + rows_n, 2)
    for f in range(2):
        rows = halo_rows(links, me, on_in, off_in, f)
        for side, link, over, under in ((0, 2, 4, 6), (1, 3, 5, 7)):
            outer, mine = (0, 2) if side == 0 else (6, 4)

            def sent(entry):
                tile = links[0, entry]
                at = jnp.maximum(tile, 0)
                chip, same = at // 2, lax.rem(at, 2) == lax.rem(me, 2)
                piece = jnp.where(same, received[chip, f], other_in[chip, f]).astype(jnp.float32)
                return jnp.where(tile >= 0, piece, 0.0)

            beside, corner_over, corner_under = sent(link), sent(over), sent(under)
            for c in range(2):
                store[f, mine + c, pl.ds(BASE, rows_n)] = own[side, f, c].astype(jnp.float32)
                store[f, outer + c, pl.ds(BASE, rows_n)] = beside[c]
                store[f, outer + c, low] = corner_over[c, rows_n - 2 : rows_n]
                store[f, outer + c, high] = corner_under[c, 0:2]
            at = 0 if side == 0 else cols_n - 16
            first = 0 if side == 0 else 14
            for where, halo in ((BASE - 2, rows[0]), (BASE + rows_n, rows[1])):
                edge = halo[:, at : at + 16].astype(jnp.float32)
                for r in range(2):
                    for c in range(2):
                        store[f, mine + c, pl.ds(where + r, 1)] = edge[r, first + c : first + c + 1]
        target = (lhs_s, lhs_c)[f]
        for column, base in enumerate((0, 1, 4, 5)):
            for a in range(3):
                for b in range(3):
                    lanes = pl.ds((3 * a + b) * chans, chans)
                    column_in = store.at[f, base + b]
                    target[pl.ds(column * span, rows_n), lanes] = column_in[
                        pl.ds(BASE - 1 + a, rows_n)
                    ].astype(jnp.bfloat16)
                    ends = [column_in[pl.ds(BASE - 2 + a, 8)], column_in[pl.ds(BASE + rows_n - 1 + a, 8)]]
                    target[pl.ds(column * span + rows_n, 16), lanes] = jnp.concatenate(ends, 0).astype(
                        jnp.bfloat16
                    )
    hidden, slope = gelu_pair(dot(lhs_s[...], w_pre[...]))
    grads = dot(lhs_c[...], w_back[...]) * slope
    valid = ((2, 4, 6), (None, 0, 1), (None, 0, 1), (3, 5, 7))
    for column in range(4):
        spans = ((0, rows_n), (rows_n, 8), (rows_n + 8, 8))
        for entry, (start, count) in zip(valid[column], spans):
            start += column * span
            piece = grads[start : start + count]
            if entry is not None:
                piece = jnp.where(links[0, entry] >= 0, piece, 0.0)
            edge_grad[pl.ds(start, count)] = piece.astype(jnp.bfloat16).astype(jnp.float32)

    def inner(values):
        return jnp.concatenate([values[span : span + rows_n], values[2 * span : 2 * span + rows_n]], 0)

    def inner_of(ref):
        return jnp.concatenate([ref[pl.ds(span, rows_n)], ref[pl.ds(2 * span, rows_n)]], 0)

    def over_cells(a, b):
        return lax.dot_general(a, b, (((0,), (0,)), ((), ())), preferred_element_type=jnp.float32)

    first_p = over_cells(inner_of(lhs_s), inner(grads).astype(jnp.bfloat16))
    second_p = over_cells(inner(hidden).astype(jnp.bfloat16), inner_of(lhs_c))
    even = lax.rem(me, 2) == 0
    for tap in range(9):
        part = slice(tap * chans, (tap + 1) * chans)
        first = first_acc[tap] + diagonal(first_p[part], mask, width)
        turned = slice((8 - tap) * chans, (9 - tap) * chans)
        second = second_acc[tap] + diagonal(second_p[:, turned], mask, width)
        keep[tap] = jnp.where(even, first, second)
        pass_on[tap] = jnp.where(even, second, first)
        size = jnp.maximum(jnp.abs(first), jnp.abs(second))
        largest = size if tap == 0 else jnp.maximum(largest, size)
    largest = jnp.max(jnp.max(largest, 0, keepdims=True), 1, keepdims=True)
    exponent = jnp.ceil(jnp.log2(jnp.maximum(largest, 2.0**-100)))
    for out in (keep, pass_on):
        out[9] = jnp.broadcast_to(exponent, out.shape[1:])


def edge_part(links, me, own, received, other_in, on_in, off_in, first_k, second_k, first_acc, second_acc):
    rows_n, chans = own.shape[3:]
    cells = 4 * (rows_n + 16)
    return pl.pallas_call(
        edge_kernel,
        in_specs=[SMEM, SMEM] + [VMEM] * 9,
        out_specs=[VMEM] * 3,
        out_shape=[
            shape_of((10,) + first_acc.shape[1:], jnp.float32),
            shape_of((10,) + first_acc.shape[1:], jnp.float32),
            shape_of((cells, chans), jnp.float32),
        ],
        scratch_shapes=[
            pltpu.VMEM((2, 8, rows_n + 32, chans), jnp.float32),
            pltpu.VMEM((cells, 9 * chans), jnp.bfloat16),
            pltpu.VMEM((cells, 9 * chans), jnp.bfloat16),
            pltpu.VMEM((9 * chans, chans), jnp.bfloat16),
            pltpu.VMEM((9 * chans, chans), jnp.bfloat16),
        ],
        compiler_params=pltpu.CompilerParams(vmem_limit_bytes=8 * MIB),
        cost_estimate=pl.CostEstimate(flops=200 << 20, bytes_accessed=3 << 20, transcendentals=1 << 15),
        name="edge",
    )(links, me, own, received, other_in, on_in, off_in, first_k, second_k, first_acc, second_acc)


def state_kernel(grad, edge_grad, first_k, cot, out, g3, w_state):
    rows_n, cols_n, chans = cot.shape
    fill_paired(w_state, first_k, same_level(first_k.shape[2], chans), True)
    span = rows_n + 16
    x = lax.broadcasted_iota(jnp.int32, (cols_n, chans), 0)
    at_left, at_right = x == 0, x == cols_n - 1

    for row in range(rows_n + 2):
        at = rows_n if row == 0 else rows_n + 8 if row == rows_n + 1 else row - 1
        ends = [edge_grad[number * span + at : number * span + at + 1] for number in range(4)]
        values = grad[row // 2, row % 2].astype(jnp.float32)
        values = jnp.where(at_left, ends[1], jnp.where(at_right, ends[2], values))
        left = jnp.where(at_left, ends[0], pltpu.roll(values, 1, 0))
        right = jnp.where(at_right, ends[3], pltpu.roll(values, cols_n - 1, 0))
        for part, piece in enumerate((left, values, right)):
            g3[row // 2, row % 2, :, part * chans : (part + 1) * chans] = piece.astype(g3.dtype)
    for pair, count in spans_of(rows_n // 2, 4):
        back = dot(windows(g3, pair, count), w_state[...])
        for row in range(2):
            piece = back[:, row * chans : (row + 1) * chans].reshape(count, cols_n, chans)
            for k in range(count):
                y = 2 * (pair + k) + row
                out[y] = (cot[y].astype(jnp.float32) + piece[k]).astype(out.dtype)


def state_part(grad, edge_grad, first_k, cot):
    rows_n, cols_n, chans = cot.shape
    return pl.pallas_call(
        state_kernel,
        in_specs=[VMEM] * 4,
        out_specs=VMEM,
        out_shape=shape_of(cot.shape, jnp.bfloat16),
        scratch_shapes=[
            pltpu.VMEM((rows_n // 2 + 1, 2, cols_n, 3 * chans), jnp.bfloat16),
            pltpu.VMEM((12 * chans, 2 * chans), jnp.bfloat16),
        ],
        compiler_params=pltpu.CompilerParams(vmem_limit_bytes=12 * MIB),
        cost_estimate=pl.CostEstimate(flops=1200 << 20, bytes_accessed=3 << 20, transcendentals=0),
        name="state",
    )(grad, edge_grad, first_k, cot)


def exchanged(value, tiles, pairs):
    both = [(a, b) for a, b in pairs if a < tiles and b < tiles]
    return lax.ppermute(value, "tiles", both + [(b, a) for a, b in both])


STATE_AT = 2
TOP = 13.0


def power(k):
    bits = (k + 126.0).astype(jnp.int32)
    value = jnp.full_like(k, 2.0**-126)
    for bit in range(8):
        half = jnp.where(bits & (1 << bit) != 0, 2.0 ** min(1 << bit, 64), 1.0)
        value = value * half * (half if bit == 7 else 1.0)
    return value


def packed(total, exponent):
    values = (total * power(TOP - exponent)).astype(jnp.float16)
    return lax.optimization_barrier(jnp.concatenate([values, exponent.astype(jnp.float16)], 0))


def unpacked(packet):
    exponent = packet[9:].astype(jnp.float32)
    return packet[:9].astype(jnp.float32) * power(exponent - TOP), exponent


def summed(keep, pass_on, me, tiles, scale, edges, state_of):
    even = lax.rem(me, 2) == 0
    if tiles & (tiles - 1):
        first, second = jnp.where(even, keep, pass_on), jnp.where(even, pass_on, keep)
        first, second = lax.psum((first[:9], second[:9]), "tiles")
        return first * scale, second * scale, state_of(edges)
    on_chip = [(t, t + 1) for t in range(0, tiles, 2)]
    other = exchanged(pass_on, tiles, on_chip)
    total, exponent = keep[:9] + other[:9], jnp.maximum(keep[9:], other[9:]) + 1.0
    distance = 2
    while distance < tiles:
        here = distance == 2 if STATE_AT == 2 else 2 * distance >= tiles
        if here:
            total, edges = lax.optimization_barrier((total, edges))
        packet = packed(total, exponent)
        other = exchanged(packet, tiles, [(t, t + distance) for t in range(tiles) if not t & distance])
        if here:
            other, state_grad = lax.optimization_barrier((other, state_of(edges)))
        (total, exponent), (more, bound) = unpacked(packet), unpacked(other)
        total, exponent = total + more, jnp.maximum(exponent, bound) + 1.0
        distance *= 2
    total = total * scale
    other = exchanged(total, tiles, on_chip)
    return jnp.where(even, total, other), jnp.where(even, other, total), state_grad


def local(ocean_state, cotangent, first_kernel, second_kernel, neighbours):
    state, cot = ocean_state[0], cotangent[0]
    rows_n, cols_n, chans = state.shape
    tiles = lax.axis_size("tiles")
    index = lax.axis_index("tiles")
    me = jnp.reshape(index, (1,)).astype(jnp.int32)
    own, send, on_out, off_out = pack(tiles // 2, neighbours, me, state, cot)
    on_chip = [(t, t + 1) for t in range(0, tiles, 2)]
    on_in = exchanged(on_out, tiles, on_chip)
    off_in = exchanged(off_out, tiles, [(t, t + 1) for t in range(1, tiles, 2)])
    cores = [list(range(core, tiles, 2)) for core in range(2)]
    received = lax.all_to_all(send, "tiles", 0, 0, axis_index_groups=cores)
    grad, first_acc, second_acc = main_part(
        neighbours, me, state, cot, on_in, off_in, first_kernel, second_kernel
    )
    received, first_acc = lax.optimization_barrier((received, first_acc))
    other_in = exchanged(received, tiles, on_chip)
    keep, pass_on, edge_grad = edge_part(
        neighbours, me, own, received, other_in, on_in, off_in, first_kernel, second_kernel, first_acc, second_acc
    )
    scale = 1.0 / math.sqrt(tiles * rows_n * cols_n)

    def state_of(edges):
        return state_part(grad, edges, first_kernel, cot)

    first, second, state_grad = summed(keep, pass_on, index, tiles, scale, edge_grad, state_of)
    shape = first_kernel.shape
    return state_grad[None], first.reshape(shape), second.reshape(shape)


def solution(mesh):
    placed = (
        P(("groups", "tiles"), None, None, None),
        P(("groups", "tiles"), None, None, None),
        P(),
        P(),
        P("tiles", None),
    )
    return jax.shard_map(
        local,
        mesh=mesh,
        in_specs=placed,
        out_specs=(
            P(("groups", "tiles"), None, None, None),
            P("groups", None, None, None),
            P("groups", None, None, None),
        ),
        check_vma=False,
    )
```

```python
import functools
import math

import jax
import jax.numpy as jnp
from jax import lax
from jax.experimental import pallas as pl
from jax.experimental.pallas import tpu as pltpu
from jax.sharding import PartitionSpec as P

CUBE = 0.044715
ROOT = math.sqrt(2.0 / math.pi)
MIB = 1 << 20
PACK = 8
SMEM = pl.BlockSpec(memory_space=pltpu.SMEM)
VMEM = pl.BlockSpec(memory_space=pltpu.VMEM)


def shape_of(dims, dtype):
    return jax.ShapeDtypeStruct(dims, dtype)


def partners(me):
    odd = lax.rem(me, 2)
    return me + 1 - 2 * odd, me - 1 + 2 * odd


def gelu_pair(v):
    square = v * v
    t = jnp.tanh(ROOT * v * (1.0 + CUBE * square))
    half = 0.5 * (1.0 + t)
    slope = half + (0.5 * ROOT) * v * (1.0 - t * t) * (1.0 + (3.0 * CUBE) * square)
    return v * half, slope


def pack_kernel(
    chips, links_in, me_ref, state, cot,
    own, send, on_out, off_out, rows, columns, links, sem, links_sem, send_sem,
):
    rows_n, cols_n, chans = state.shape
    me = me_ref[0]
    copies = [pltpu.make_async_copy(links_in, links, links_sem)]
    for f, field in enumerate((state, cot)):
        for side in range(2):
            beside = field.at[:, pl.ds(side * (cols_n - 16), 16)]
            copies.append(pltpu.make_async_copy(beside, columns.at[f, side], sem.at[f, side]))
            outer = field.at[pl.ds(side * (rows_n - 2), 2)]
            copies.append(pltpu.make_async_copy(outer, rows.at[f, side], sem.at[f, 2 + side]))
    for copy in copies:
        copy.start()
    for copy in copies:
        copy.wait()
    for f in range(2):
        for side, first in ((0, 0), (1, 14)):
            values = columns[f, side].astype(jnp.float32)
            for c in range(2):
                own[side, f, c] = values[:, first + c, :].astype(jnp.bfloat16)
    copies = []
    for j in range(chips):
        side = jnp.where(2 * j + 1 > me, 1, 0)
        copies.append(pltpu.make_async_copy(own.at[side], send.at[j], send_sem.at[j]))
        copies[-1].start()
    for target, out in zip(partners(me), (on_out, off_out)):
        for f in range(2):
            top, bottom = rows[f, 0], rows[f, 1]
            sent = jnp.where(links[0, 1] == target, bottom, jnp.zeros_like(bottom))
            out[2 * f : 2 * f + 2] = jnp.where(links[0, 0] == target, top, sent)
    for copy in copies:
        copy.wait()


def pack(chips, links, me, state, cot):
    rows_n, cols_n, chans = state.shape
    far = pl.BlockSpec(memory_space=pltpu.HBM)
    placed = functools.partial(pltpu.with_memory_space_constraint, memory_space=pltpu.HBM)
    return pl.pallas_call(
        functools.partial(pack_kernel, chips),
        in_specs=[far, SMEM, far, far],
        out_specs=[VMEM, far, VMEM, VMEM],
        out_shape=[
            shape_of((2, 2, 2, rows_n, chans), jnp.bfloat16),
            pltpu.HBM((chips, 2, 2, rows_n, chans), jnp.bfloat16),
            shape_of((4, cols_n, chans), jnp.bfloat16),
            shape_of((4, cols_n, chans), jnp.bfloat16),
        ],
        scratch_shapes=[
            pltpu.VMEM((2, 2, 2, cols_n, chans), jnp.bfloat16),
            pltpu.VMEM((2, 2, rows_n, 16, chans), jnp.bfloat16),
            pltpu.SMEM(links.shape, links.dtype),
            pltpu.SemaphoreType.DMA((2, 4)),
            pltpu.SemaphoreType.DMA,
            pltpu.SemaphoreType.DMA((chips,)),
        ],
        compiler_params=pltpu.CompilerParams(vmem_limit_bytes=PACK * MIB),
        name="pack",
    )(placed(links), me, placed(state), placed(cot))


def halo_rows(links, me, on_in, off_in, f):
    found = []
    for link in (0, 1):
        rows = jnp.zeros((2,) + off_in.shape[1:], off_in.dtype)
        for source, packet in zip(partners(me), (on_in, off_in)):
            rows = jnp.where(links[0, link] == source, packet[2 * f : 2 * f + 2], rows)
        found.append(rows)
    return found


def same_level(width, chans):
    down = lax.broadcasted_iota(jnp.int32, (chans, chans), 0) // width
    across = lax.broadcasted_iota(jnp.int32, (chans, chans), 1) // width
    return down == across


def diagonal(product, mask, width):
    kept = jnp.where(mask, product, 0.0)
    return sum(kept[at : at + width] for at in range(0, product.shape[0], width))


def thirds(ref, row, values):
    count, cols_n, chans = values.shape
    flat = values.reshape(count * cols_n, chans).astype(jnp.float32)
    left = pltpu.roll(flat, 1, 0).astype(ref.dtype)
    right = pltpu.roll(flat, count * cols_n - 1, 0).astype(ref.dtype)
    for part, piece in enumerate((left, values, right)):
        lanes = slice(part * chans, (part + 1) * chans)
        ref[pl.ds(row // 2, count // 2), :, :, lanes] = piece.reshape(count // 2, 2, cols_n, chans)


def windows(ref, pair, count):
    parts = []
    for row in range(4):
        rows = ref[pl.ds(pair + row // 2, count), row % 2]
        parts.append(rows.reshape(count * rows.shape[1], rows.shape[2]))
    return jnp.concatenate(parts, 1)


def dot(a, b):
    return jnp.dot(a, b, preferred_element_type=jnp.float32)


def spans_of(total, most):
    count = pl.cdiv(total, most)
    bounds = [total * i // count for i in range(count + 1)]
    return [(lo, hi - lo) for lo, hi in zip(bounds, bounds[1:])]


def level_blocks(kernel, tap, mask):
    block = kernel[tap // 3, tap % 3].astype(jnp.float32)
    return jnp.where(mask, jnp.concatenate([block] * (mask.shape[0] // block.shape[0]), 0), 0.0)


def fill_paired(ref, kernel, mask, turned):
    chans = mask.shape[0]
    none = jnp.zeros((3 * chans, chans), ref.dtype)
    ref[9 * chans : 12 * chans, 0:chans] = none
    ref[0 : 3 * chans, chans : 2 * chans] = none
    for tap in range(9):
        dense = level_blocks(kernel, tap, mask)
        if turned:
            paired(ref, 8 - tap, dense.T.astype(ref.dtype))
        else:
            paired(ref, tap, dense.astype(ref.dtype))


def paired(ref, tap, dense):
    chans = dense.shape[0]
    for row in range(2):
        ref[pl.ds((tap + 3 * row) * chans, chans), row * chans : (row + 1) * chans] = dense


def main_kernel(
    links, me_ref, state, cot, on_in, off_in, first_k, second_k,
    grad, first_acc, second_acc,
    w_pre, w_back, s3, c3, acc1, acc2, grad_v, sem,
):
    me = me_ref[0]
    rows_n, cols_n, chans = state.shape
    width = first_k.shape[2]
    mask = same_level(width, chans)
    fill_paired(w_pre, first_k, mask, False)
    fill_paired(w_back, second_k, mask, True)
    for f, (field, store) in enumerate(((state, s3), (cot, c3))):
        above, below = halo_rows(links, me, on_in, off_in, f)
        thirds(store, 0, above)
        thirds(store, rows_n + 2, below)
        for row, count in spans_of(rows_n // 2, 4):
            thirds(store, 2 * row + 2, field[pl.ds(2 * row, 2 * count)])

    pairs_n = rows_n // 2 + 1
    def products(pair, grads, hidden, near_state, near_cot):
        one, two = dot(grads.T, near_state), dot(hidden.T, near_cot)
        if pair == 0:
            acc1[...] = one
            acc2[...] = two
        else:
            acc1[...] += one
            acc2[...] += two

    copies = []
    later = None
    for k, (pair, count) in enumerate(spans_of(pairs_n, PAIRS)):
        near_state, near_cot = windows(s3, pair, count), windows(c3, pair, count)
        pre, back = dot(near_state, w_pre[...]), dot(near_cot, w_back[...])
        if later is not None:
            products(*later)
        hidden, slope = gelu_pair(pre)
        grads = back * slope
        cell = lax.broadcasted_iota(jnp.int32, grads.shape, 0)
        lane = lax.broadcasted_iota(jnp.int32, grads.shape, 1)
        x = lax.rem(cell, cols_n)
        inner = (x > 0) & (x < cols_n - 1)
        if pair == 0:
            outside = (cell < cols_n) & (lane < chans)
            inner = inner & ~outside
            grads = jnp.where(outside & (links[0, 0] < 0), 0.0, grads)
        if pair + count == pairs_n:
            outside = (cell >= (count - 1) * cols_n) & (lane >= chans)
            inner = inner & ~outside
            grads = jnp.where(outside & (links[0, 1] < 0), 0.0, grads)
        for row in range(2):
            piece = grads[:, row * chans : (row + 1) * chans].astype(jnp.bfloat16)
            grad_v[pl.ds(pair, count), row] = piece.reshape(count, cols_n, chans)
        part = pl.ds(pair, count)
        copies.append(pltpu.make_async_copy(grad_v.at[part], grad.at[part], sem.at[k]))
        copies[-1].start()
        grads = jnp.where(inner, grads, 0.0).astype(jnp.bfloat16)
        hidden = jnp.where(inner, hidden, 0.0).astype(jnp.bfloat16)
        later = (pair, grads, hidden, near_state, near_cot)
    products(*later)
    for tap in range(9):
        one, two = (slice((tap + 3 * r) * chans, (tap + 3 * r + 1) * chans) for r in range(2))
        first = acc1[0:chans, one] + acc1[chans : 2 * chans, two]
        second = acc2[0:chans, one] + acc2[chans : 2 * chans, two]
        first_acc[tap] = diagonal(first.T, mask, width)
        second_acc[8 - tap] = diagonal(second, mask, width)
    for copy in copies:
        copy.wait()


PAIRS = 6


def main_part(links, me, state, cot, on_in, off_in, first_k, second_k):
    rows_n, cols_n, chans = state.shape
    width = first_k.shape[2]
    flops = 2 * rows_n * cols_n * 9 * chans * chans * 4
    return pl.pallas_call(
        main_kernel,
        in_specs=[SMEM, SMEM] + [VMEM] * 6,
        out_specs=[pl.BlockSpec(memory_space=pltpu.HBM), VMEM, VMEM],
        out_shape=[
            pltpu.HBM((rows_n // 2 + 1, 2, cols_n, chans), jnp.bfloat16),
            shape_of((9, width, chans), jnp.float32),
            shape_of((9, width, chans), jnp.float32),
        ],
        scratch_shapes=[
            pltpu.VMEM((12 * chans, 2 * chans), jnp.bfloat16),
            pltpu.VMEM((12 * chans, 2 * chans), jnp.bfloat16),
            pltpu.VMEM((rows_n // 2 + 2, 2, cols_n, 3 * chans), jnp.bfloat16),
            pltpu.VMEM((rows_n // 2 + 2, 2, cols_n, 3 * chans), jnp.bfloat16),
            pltpu.VMEM((2 * chans, 12 * chans), jnp.float32),
            pltpu.VMEM((2 * chans, 12 * chans), jnp.float32),
            pltpu.VMEM((rows_n // 2 + 1, 2, cols_n, chans), jnp.bfloat16),
            pltpu.SemaphoreType.DMA((len(spans_of(rows_n // 2 + 1, PAIRS)),)),
        ],
        compiler_params=pltpu.CompilerParams(vmem_limit_bytes=26 * MIB),
        cost_estimate=pl.CostEstimate(flops=20 * flops, bytes_accessed=5 << 20, transcendentals=1 << 19),
        name="main",
    )(links, me, state, cot, on_in, off_in, first_k, second_k)


BASE = 16


def edge_kernel(
    links, me_ref, own, received, other_in, on_in, off_in, first_k, second_k, first_acc, second_acc,
    keep, pass_on, edge_grad, store, lhs_s, lhs_c, w_pre, w_back,
):
    me = me_ref[0]
    rows_n, chans = own.shape[3], own.shape[4]
    cols_n = off_in.shape[1]
    width = first_acc.shape[1]
    span = rows_n + 16
    mask = same_level(width, chans)
    for tap in range(9):
        at = slice(tap * chans, (tap + 1) * chans)
        w_pre[at] = level_blocks(first_k, tap, mask).astype(w_pre.dtype)
        w_back[at] = level_blocks(second_k, 8 - tap, mask).T.astype(w_back.dtype)
    store[...] = jnp.zeros_like(store)
    low, high = pl.ds(BASE - 2, 2), pl.ds(BASE + rows_n, 2)
    for f in range(2):
        rows = halo_rows(links, me, on_in, off_in, f)
        for side, link, over, under in ((0, 2, 4, 6), (1, 3, 5, 7)):
            outer, mine = (0, 2) if side == 0 else (6, 4)

            def sent(entry):
                tile = links[0, entry]
                at = jnp.maximum(tile, 0)
                chip, same = at // 2, lax.rem(at, 2) == lax.rem(me, 2)
                piece = jnp.where(same, received[chip, f], other_in[chip, f]).astype(jnp.float32)
                return jnp.where(tile >= 0, piece, 0.0)

            beside, corner_over, corner_under = sent(link), sent(over), sent(under)
            for c in range(2):
                store[f, mine + c, pl.ds(BASE, rows_n)] = own[side, f, c].astype(jnp.float32)
                store[f, outer + c, pl.ds(BASE, rows_n)] = beside[c]
                store[f, outer + c, low] = corner_over[c, rows_n - 2 : rows_n]
                store[f, outer + c, high] = corner_under[c, 0:2]
            at = 0 if side == 0 else cols_n - 16
            first = 0 if side == 0 else 14
            for where, halo in ((BASE - 2, rows[0]), (BASE + rows_n, rows[1])):
                edge = halo[:, at : at + 16].astype(jnp.float32)
                for r in range(2):
                    for c in range(2):
                        store[f, mine + c, pl.ds(where + r, 1)] = edge[r, first + c : first + c + 1]
        target = (lhs_s, lhs_c)[f]
        for column, base in enumerate((0, 1, 4, 5)):
            for a in range(3):
                for b in range(3):
                    lanes = pl.ds((3 * a + b) * chans, chans)
                    column_in = store.at[f, base + b]
                    target[pl.ds(column * span, rows_n), lanes] = column_in[
                        pl.ds(BASE - 1 + a, rows_n)
                    ].astype(jnp.bfloat16)
                    ends = [column_in[pl.ds(BASE - 2 + a, 8)], column_in[pl.ds(BASE + rows_n - 1 + a, 8)]]
                    target[pl.ds(column * span + rows_n, 16), lanes] = jnp.concatenate(ends, 0).astype(
                        jnp.bfloat16
                    )
    hidden, slope = gelu_pair(dot(lhs_s[...], w_pre[...]))
    grads = dot(lhs_c[...], w_back[...]) * slope
    valid = ((2, 4, 6), (None, 0, 1), (None, 0, 1), (3, 5, 7))
    for column in range(4):
        spans = ((0, rows_n), (rows_n, 8), (rows_n + 8, 8))
        for entry, (start, count) in zip(valid[column], spans):
            start += column * span
            piece = grads[start : start + count]
            if entry is not None:
                piece = jnp.where(links[0, entry] >= 0, piece, 0.0)
            edge_grad[pl.ds(start, count)] = piece.astype(jnp.bfloat16).astype(jnp.float32)

    def inner(values):
        return jnp.concatenate([values[span : span + rows_n], values[2 * span : 2 * span + rows_n]], 0)

    def inner_of(ref):
        return jnp.concatenate([ref[pl.ds(span, rows_n)], ref[pl.ds(2 * span, rows_n)]], 0)

    def over_cells(a, b):
        return lax.dot_general(a, b, (((0,), (0,)), ((), ())), preferred_element_type=jnp.float32)

    first_p = over_cells(inner_of(lhs_s), inner(grads).astype(jnp.bfloat16))
    second_p = over_cells(inner(hidden).astype(jnp.bfloat16), inner_of(lhs_c))
    even = lax.rem(me, 2) == 0
    for tap in range(9):
        part = slice(tap * chans, (tap + 1) * chans)
        first = first_acc[tap] + diagonal(first_p[part], mask, width)
        turned = slice((8 - tap) * chans, (9 - tap) * chans)
        second = second_acc[tap] + diagonal(second_p[:, turned], mask, width)
        keep[tap] = jnp.where(even, first, second)
        pass_on[tap] = jnp.where(even, second, first)
        size = jnp.maximum(jnp.abs(first), jnp.abs(second))
        largest = size if tap == 0 else jnp.maximum(largest, size)
    largest = jnp.max(jnp.max(largest, 0, keepdims=True), 1, keepdims=True)
    exponent = jnp.ceil(jnp.log2(jnp.maximum(largest, 2.0**-100)))
    for out in (keep, pass_on):
        out[9] = jnp.broadcast_to(exponent, out.shape[1:])


def edge_part(links, me, own, received, other_in, on_in, off_in, first_k, second_k, first_acc, second_acc):
    rows_n, chans = own.shape[3:]
    cells = 4 * (rows_n + 16)
    return pl.pallas_call(
        edge_kernel,
        in_specs=[SMEM, SMEM] + [VMEM] * 9,
        out_specs=[VMEM] * 3,
        out_shape=[
            shape_of((10,) + first_acc.shape[1:], jnp.float32),
            shape_of((10,) + first_acc.shape[1:], jnp.float32),
            shape_of((cells, chans), jnp.float32),
        ],
        scratch_shapes=[
            pltpu.VMEM((2, 8, rows_n + 32, chans), jnp.float32),
            pltpu.VMEM((cells, 9 * chans), jnp.bfloat16),
            pltpu.VMEM((cells, 9 * chans), jnp.bfloat16),
            pltpu.VMEM((9 * chans, chans), jnp.bfloat16),
            pltpu.VMEM((9 * chans, chans), jnp.bfloat16),
        ],
        compiler_params=pltpu.CompilerParams(vmem_limit_bytes=8 * MIB),
        cost_estimate=pl.CostEstimate(flops=200 << 20, bytes_accessed=3 << 20, transcendentals=1 << 15),
        name="edge",
    )(links, me, own, received, other_in, on_in, off_in, first_k, second_k, first_acc, second_acc)


def state_kernel(grad, edge_grad, first_k, cot, out, g3, w_state):
    rows_n, cols_n, chans = cot.shape
    fill_paired(w_state, first_k, same_level(first_k.shape[2], chans), True)
    span = rows_n + 16
    x = lax.broadcasted_iota(jnp.int32, (cols_n, chans), 0)
    at_left, at_right = x == 0, x == cols_n - 1

    for row in range(rows_n + 2):
        at = rows_n if row == 0 else rows_n + 8 if row == rows_n + 1 else row - 1
        ends = [edge_grad[number * span + at : number * span + at + 1] for number in range(4)]
        values = grad[row // 2, row % 2].astype(jnp.float32)
        values = jnp.where(at_left, ends[1], jnp.where(at_right, ends[2], values))
        left = jnp.where(at_left, ends[0], pltpu.roll(values, 1, 0))
        right = jnp.where(at_right, ends[3], pltpu.roll(values, cols_n - 1, 0))
        for part, piece in enumerate((left, values, right)):
            g3[row // 2, row % 2, :, part * chans : (part + 1) * chans] = piece.astype(g3.dtype)
    for pair, count in spans_of(rows_n // 2, 4):
        back = dot(windows(g3, pair, count), w_state[...])
        for row in range(2):
            piece = back[:, row * chans : (row + 1) * chans].reshape(count, cols_n, chans)
            for k in range(count):
                y = 2 * (pair + k) + row
                out[y] = (cot[y].astype(jnp.float32) + piece[k]).astype(out.dtype)


def state_part(grad, edge_grad, first_k, cot):
    rows_n, cols_n, chans = cot.shape
    return pl.pallas_call(
        state_kernel,
        in_specs=[VMEM] * 4,
        out_specs=VMEM,
        out_shape=shape_of(cot.shape, jnp.bfloat16),
        scratch_shapes=[
            pltpu.VMEM((rows_n // 2 + 1, 2, cols_n, 3 * chans), jnp.bfloat16),
            pltpu.VMEM((12 * chans, 2 * chans), jnp.bfloat16),
        ],
        compiler_params=pltpu.CompilerParams(vmem_limit_bytes=12 * MIB),
        cost_estimate=pl.CostEstimate(flops=1200 << 20, bytes_accessed=3 << 20, transcendentals=0),
        name="state",
    )(grad, edge_grad, first_k, cot)


def exchanged(value, tiles, pairs):
    both = [(a, b) for a, b in pairs if a < tiles and b < tiles]
    return lax.ppermute(value, "tiles", both + [(b, a) for a, b in both])


STATE_AT = 8
TOP = 13.0


def power(k):
    bits = (k + 126.0).astype(jnp.int32)
    value = jnp.full_like(k, 2.0**-126)
    for bit in range(8):
        half = jnp.where(bits & (1 << bit) != 0, 2.0 ** min(1 << bit, 64), 1.0)
        value = value * half * (half if bit == 7 else 1.0)
    return value


def packed(total, exponent):
    values = (total * power(TOP - exponent)).astype(jnp.float16)
    return lax.optimization_barrier(jnp.concatenate([values, exponent.astype(jnp.float16)], 0))


def unpacked(packet):
    exponent = packet[9:].astype(jnp.float32)
    return packet[:9].astype(jnp.float32) * power(exponent - TOP), exponent


def summed(keep, pass_on, me, tiles, scale, edges, state_of):
    even = lax.rem(me, 2) == 0
    if tiles & (tiles - 1):
        first, second = jnp.where(even, keep, pass_on), jnp.where(even, pass_on, keep)
        first, second = lax.psum((first[:9], second[:9]), "tiles")
        return first * scale, second * scale, state_of(edges)
    on_chip = [(t, t + 1) for t in range(0, tiles, 2)]
    other = exchanged(pass_on, tiles, on_chip)
    total, exponent = keep[:9] + other[:9], jnp.maximum(keep[9:], other[9:]) + 1.0
    distance = 2
    while distance < tiles:
        here = distance == 2 if STATE_AT == 2 else 2 * distance >= tiles
        if here:
            total, edges = lax.optimization_barrier((total, edges))
        packet = packed(total, exponent)
        other = exchanged(packet, tiles, [(t, t + distance) for t in range(tiles) if not t & distance])
        if here:
            other, state_grad = lax.optimization_barrier((other, state_of(edges)))
        (total, exponent), (more, bound) = unpacked(packet), unpacked(other)
        total, exponent = total + more, jnp.maximum(exponent, bound) + 1.0
        distance *= 2
    total = total * scale
    other = exchanged(total, tiles, on_chip)
    return jnp.where(even, total, other), jnp.where(even, other, total), state_grad


def local(ocean_state, cotangent, first_kernel, second_kernel, neighbours):
    state, cot = ocean_state[0], cotangent[0]
    rows_n, cols_n, chans = state.shape
    tiles = lax.axis_size("tiles")
    index = lax.axis_index("tiles")
    me = jnp.reshape(index, (1,)).astype(jnp.int32)
    own, send, on_out, off_out = pack(tiles // 2, neighbours, me, state, cot)
    on_chip = [(t, t + 1) for t in range(0, tiles, 2)]
    on_in = exchanged(on_out, tiles, on_chip)
    off_in = exchanged(off_out, tiles, [(t, t + 1) for t in range(1, tiles, 2)])
    cores = [list(range(core, tiles, 2)) for core in range(2)]
    received = lax.all_to_all(send, "tiles", 0, 0, axis_index_groups=cores)
    grad, first_acc, second_acc = main_part(
        neighbours, me, state, cot, on_in, off_in, first_kernel, second_kernel
    )
    received, first_acc = lax.optimization_barrier((received, first_acc))
    other_in = exchanged(received, tiles, on_chip)
    keep, pass_on, edge_grad = edge_part(
        neighbours, me, own, received, other_in, on_in, off_in, first_kernel, second_kernel, first_acc, second_acc
    )
    scale = 1.0 / math.sqrt(tiles * rows_n * cols_n)

    def state_of(edges):
        return state_part(grad, edges, first_kernel, cot)

    first, second, state_grad = summed(keep, pass_on, index, tiles, scale, edge_grad, state_of)
    shape = first_kernel.shape
    return state_grad[None], first.reshape(shape), second.reshape(shape)


def solution(mesh):
    placed = (
        P(("groups", "tiles"), None, None, None),
        P(("groups", "tiles"), None, None, None),
        P(),
        P(),
        P("tiles", None),
    )
    return jax.shard_map(
        local,
        mesh=mesh,
        in_specs=placed,
        out_specs=(
            P(("groups", "tiles"), None, None, None),
            P("groups", None, None, None),
            P("groups", None, None, None),
        ),
        check_vma=False,
    )
```
